256 devices in a mesh: occ: 16 (over z_hi, y), fit: 16 (over x, z_lo, core).
Axes of the slice: x: 4, y: 4, z: 8 (z_hi: 4, z_lo: 2; z = z_hi * 2 + z_lo), core: 2. Of those that a mesh axis runs over, the one named last changes fastest.
Arguments:
- integrals: bfloat16 [8192, 16, 512], P('fit', 'occ'), may hold values from -0.62890625 to 0.62890625
- fitting: bfloat16 [8192, 8192], P('fit', 'occ'), may hold values from -0.1 to 1.1
- occ_energy: float32 [16], P('occ'), may hold values from -2 to -0.5
- vir_energy: float32 [512], replicated, may hold values from 0.2 to 3
Outputs:
- density: float32 [8192, 16, 512], P('fit', 'occ')
- pair_energy: float32 [16, 6], P('occ')
The draws below stay inside these ranges and needn't reach their ends.
All inputs are finite; a program needn't handle non-finite values.
Results may differ from the reference program's by a relative error of at most 0.0003.
Values may be sent and summed in bfloat16 or wider, within the bound.
A program may use at most 64 MiB of HBM per device.

```python
import math
import jax
import jax.numpy as jnp
from jax import lax

NVIR = 512
STOPS = 6
NAUX = 8192
NOCC = 16


def draw_fitting(key, part):
    offdiag = jax.random.normal(key, (NAUX, NAUX), jnp.float32) * (0.6 / math.sqrt(NAUX))
    offdiag = jnp.clip(offdiag, -0.09, 0.09)
    return (offdiag + jnp.eye(NAUX, dtype=jnp.float32)).astype(jnp.bfloat16)


def level_of(stream_key, extent, split, smallest, high):
    factor_of = 1.0
    for axis_at, blocks in split:
        draws = jax.random.uniform(jax.random.fold_in(jax.random.fold_in(stream_key, 6), axis_at), (blocks,), jnp.float32, smallest / len(split), high / len(split))
        factor_of = factor_of * jnp.repeat(jnp.exp(draws), extent[axis_at] // blocks).reshape((-1,) + (1,) * (len(extent) - 1 - axis_at))
    return factor_of


def gaussian(stream_key, shape, scale, most, cuts=(), kind=jnp.bfloat16):
    array = jax.random.normal(stream_key, shape, jnp.float32) * scale
    if len(cuts) > 0:
        array = level_of(stream_key, shape, cuts, -0.22, 0.18) * array
    return jnp.clip(array, min=-most, max=most).astype(kind)


def setup_inputs(seed: int = 0) -> dict:
    arg_keys = jax.random.split(jax.random.key(seed), 5)
    integrals = gaussian(arg_keys[0], (NAUX, NOCC, NVIR), (NAUX ** -0.25), 0.62890625, ((0, 16), (1, 16)))
    fitting = draw_fitting(jax.random.fold_in(arg_keys[4], 71), 0)
    occ_energy = jnp.clip(-2.0 + 1.5 * jax.random.uniform(arg_keys[2], (NOCC,), jnp.float32) ** level_of(arg_keys[2], (NOCC,), ((0, 16),), -0.2, 0.2), -2.0, -0.5)
    vir_energy = jnp.clip(jax.random.uniform(arg_keys[3], (NVIR,), jnp.float32, 0.2, 3.0), 0.2, 3.0)
    return {"integrals": integrals, "fitting": fitting, "occ_energy": occ_energy, "vir_energy": vir_energy}


def reference(integrals, fitting, occ_energy, vir_energy):
    flat = integrals.astype(jnp.float32).reshape(NAUX, NOCC * NVIR)
    fitted = jnp.dot(fitting.astype(jnp.float32), flat, precision=lax.Precision.HIGHEST, preferred_element_type=jnp.float32).reshape(NAUX, NOCC, NVIR)

    def one_orbital(index):
        own = lax.dynamic_index_in_dim(fitted, index, 1, keepdims=False)
        own_energy = lax.dynamic_index_in_dim(occ_energy, index, 0, keepdims=False)
        total = jnp.zeros((NAUX, NVIR), jnp.float32)
        energies = []
        for step in range(STOPS):
            partner = ((index + step) % NOCC).astype(jnp.int32)
            other = lax.dynamic_index_in_dim(fitted, partner, 1, keepdims=False)
            other_energy = lax.dynamic_index_in_dim(occ_energy, partner, 0, keepdims=False)
            pair = lax.dot_general(own, other, (((0,), (0,)), ((), ())), precision=lax.Precision.HIGHEST, preferred_element_type=jnp.float32)
            denom = own_energy + other_energy - vir_energy[:, None] - vir_energy[None, :]
            amplitude = pair / denom
            energies.append(jnp.sum(amplitude * (2.0 * pair - pair.T)) / (NVIR * NVIR))
            total = total + jnp.dot(other, amplitude.T, precision=lax.Precision.HIGHEST, preferred_element_type=jnp.float32)
        return total, jnp.stack(energies)

    totals, pair_energy = lax.map(one_orbital, jnp.arange(NOCC, dtype=jnp.int32))
    density = jnp.transpose(totals, (1, 0, 2))
    return density, pair_energy
```

```python
import functools

import jax
import jax.numpy as jnp
from jax import lax
from jax.experimental import pallas as pl
from jax.experimental.pallas import tpu as pltpu
from jax.sharding import PartitionSpec as P

STOPS = 6
MESH = pl.DeviceIdType.MESH
HALVES = (pl.ds(0, 256), pl.ds(256, 256))


class Place:
    def __init__(self):
        self.occ = lax.axis_index("occ")
        self.fit = lax.axis_index("fit")
        self.z, self.y = self.occ // 4, self.occ % 4
        self.x, self.low, self.core = self.fit // 4, (self.fit // 2) % 2, self.fit % 2

    def o(self, dz, dy):
        return ((self.z + dz + 4) % 4) * 4 + (self.y + dy + 4) % 4

    def f(self, dx, flip_low=0, flip_core=0):
        low = self.low if not flip_low else 1 - self.low
        core = self.core if not flip_core else 1 - self.core
        return ((self.x + dx + 4) % 4) * 4 + low * 2 + core


def entry_barrier(peers):
    barrier = pltpu.get_barrier_semaphore()
    for occ, fit in peers:
        pl.semaphore_signal(barrier, inc=1, device_id={"occ": occ, "fit": fit}, device_id_type=MESH)
    pl.semaphore_wait(barrier, len(peers))


def fit_kernel(fit_ref, int_ref, out_ref, fb, ib, fsend, frecv, isend, irecv):
    at = Place()
    me = (at.occ, at.fit)
    entry_barrier(
        [(at.o(dz, dy), at.fit) for dz, dy in ((1, 0), (-1, 0), (0, 1), (0, -1))]
        + [(at.occ, at.f(1)), (at.occ, at.f(-1)), (at.occ, at.f(0, 1)), (at.occ, at.f(0, 0, 1))]
    )
    started = []

    def send(buf, recv, sends, src, slot, half, occ, fit):
        at_half = () if half is None else (HALVES[half],)
        sem = sends.at[len(started)]
        copy = pltpu.make_async_remote_copy(
            src_ref=src.at[at_half] if half is not None else src,
            dst_ref=buf.at[(slot,) + at_half],
            send_sem=sem,
            recv_sem=recv.at[slot, 0 if half is None else half],
            device_id={"occ": occ, "fit": fit},
            device_id_type=MESH,
        )
        copy.start()
        started.append(copy)

    def arrived(buf, recv, slot, half):
        part = buf.at[slot] if half is None else buf.at[slot, HALVES[half]]
        pltpu.make_async_remote_copy(
            src_ref=part,
            dst_ref=part,
            send_sem=fsend.at[0],
            recv_sem=recv.at[slot, 0 if half is None else half],
            device_id={"occ": me[0], "fit": me[1]},
            device_id_type=MESH,
        ).wait_recv()

    def fsnd(src, slot, half, dz, dy):
        send(fb, frecv, fsend, src, slot, half, at.o(dz, dy), at.fit)

    def isnd(src, slot, half, fit):
        send(ib, irecv, fsend, src, slot, half, at.occ, fit)

    def f_got(dz, dy):
        slot = at.o(dz, dy)
        if dz == 2 and dy == 0 or dy == 2:
            arrived(fb, frecv, slot, 0)
            arrived(fb, frecv, slot, 1)
        else:
            arrived(fb, frecv, slot, None)
        return slot

    def i_got(dx, flip_low):
        slot = at.f(dx, flip_low)
        if dx == 2:
            arrived(ib, irecv, slot, 0)
            arrived(ib, irecv, slot, 1)
        else:
            arrived(ib, irecv, slot, None)
        return slot

    def f_spread(dz):
        slot = at.o(dz, 0)
        src = fit_ref if dz == 0 else fb.at[slot]
        fsnd(src, slot, None, 0, 1)
        fsnd(src, slot, None, 0, -1)

    def f_relay_y(dz):
        slot = f_got(dz, 1)
        fsnd(fb.at[slot], slot, 0, 0, -1)
        slot = f_got(dz, -1)
        fsnd(fb.at[slot], slot, 1, 0, 1)

    def to_core(src, slot):
        isnd(src, slot, None, at.f(0, 0, 1))

    def i_spread(flip_low):
        slot = at.f(0, flip_low)
        src = ib.at[slot] if flip_low else int_ref
        isnd(src, slot, None, at.f(1))
        isnd(src, slot, None, at.f(-1))

    def i_relay(flip_low):
        slot = i_got(1, flip_low)
        isnd(ib.at[slot], slot, 0, at.f(-1))
        to_core(ib.at[slot], slot)
        slot = i_got(-1, flip_low)
        isnd(ib.at[slot], slot, 1, at.f(1))
        to_core(ib.at[slot], slot)

    def multiply(dy):
        for dz in (0, 1, -1, 2):
            if dy == 2:
                f_got(dz, 2)

        def one(k, carry):
            slot = at.o(k, dy)
            out_ref[...] += jnp.dot(fb[slot], ib[slot], preferred_element_type=jnp.float32)
            return carry

        lax.fori_loop(0, 4, one, 0)

    fsnd(fit_ref, at.occ, None, 1, 0)
    fsnd(fit_ref, at.occ, None, -1, 0)
    f_spread(0)
    i_spread(0)
    to_core(int_ref, at.fit)
    fb[at.occ] = fit_ref[...]
    ib[at.fit] = int_ref[...]
    out_ref[...] = jnp.zeros_like(out_ref)

    f_relay_y(0)
    i_relay(0)
    slot = i_got(2, 0)
    to_core(ib.at[slot], slot)
    slot = f_got(1, 0)
    fsnd(fb.at[slot], slot, 0, -1, 0)
    f_spread(1)
    slot = f_got(-1, 0)
    fsnd(fb.at[slot], slot, 1, 1, 0)
    f_spread(-1)
    isnd(int_ref, at.fit, None, at.f(0, 1))
    f_got(2, 0)
    f_spread(2)
    slot = i_got(0, 1)
    i_spread(1)
    to_core(ib.at[slot], slot)
    f_relay_y(1)
    i_relay(1)
    f_relay_y(-1)
    slot = i_got(2, 1)
    to_core(ib.at[slot], slot)
    f_relay_y(2)
    for flip_low in (0, 1):
        for dx in (0, 1, -1, 2):
            arrived(ib, irecv, at.f(dx, flip_low, 1), None)
    multiply(0)
    multiply(1)
    multiply(3)
    multiply(2)
    for copy in started:
        copy.wait_send()


def fitted_of(fitting, integrals):
    sends = 37
    return pl.pallas_call(
        fit_kernel,
        out_shape=jax.ShapeDtypeStruct((512, 512), jnp.float32),
        in_specs=[pl.BlockSpec(memory_space=pltpu.VMEM)] * 2,
        out_specs=pl.BlockSpec(memory_space=pltpu.VMEM),
        scratch_shapes=[
            pltpu.VMEM((16, 512, 512), jnp.bfloat16),
            pltpu.VMEM((16, 512, 512), jnp.bfloat16),
            pltpu.SemaphoreType.DMA((sends,)),
            pltpu.SemaphoreType.DMA((16, 2)),
            pltpu.SemaphoreType.DMA((1,)),
            pltpu.SemaphoreType.DMA((16, 2)),
        ],
        compiler_params=pltpu.CompilerParams(
            collective_id=0, has_side_effects=True, vmem_limit_bytes=40 * 1024 * 1024
        ),
    )(fitting, integrals)


def passed_along(block, axis, distance):
    devices = range(lax.axis_size(axis))
    route = [((i - distance) % len(devices), i) for i in devices]
    return lax.ppermute(block, axis, route)


def body(integrals, fitting, occ_energy, vir_energy):
    nvir = integrals.shape[2]
    fitted = fitted_of(fitting, integrals[:, 0, :])
    own_energy = occ_energy[0]
    partner = fitted
    partner_energy = occ_energy
    density = jnp.zeros_like(fitted)
    energies = []
    for step in range(STOPS):
        if step > 0:
            partner, partner_energy = passed_along((partner, partner_energy), "occ", -1)
        local_pair = lax.dot_general(
            fitted,
            partner,
            (((0,), (0,)), ((), ())),
            precision=lax.Precision.HIGHEST,
            preferred_element_type=jnp.float32,
        )
        denom = own_energy + partner_energy[0] - vir_energy[:, None] - vir_energy[None, :]
        summed = lax.psum(local_pair, "fit")
        amplitude = summed / denom
        energies.append(jnp.sum(amplitude * (2.0 * summed - summed.T)) / (nvir * nvir))
        density = density + jnp.dot(
            partner,
            amplitude.T,
            precision=lax.Precision.HIGHEST,
            preferred_element_type=jnp.float32,
        )
    pair_energy = jnp.stack(energies)[None, :]
    return (density[:, None, :], pair_energy)


def solution(mesh):
    placed = (P("fit", "occ", None), P("fit", "occ"), P("occ"), P())
    return jax.shard_map(
        body,
        mesh=mesh,
        in_specs=placed,
        out_specs=(P("fit", "occ", None), P("occ", None)),
        check_vma=False,
    )
```

```python
import functools

import jax
import jax.numpy as jnp
from jax import lax
from jax.experimental import pallas as pl
from jax.experimental.pallas import tpu as pltpu
from jax.sharding import PartitionSpec as P

STOPS = 6
MESH = pl.DeviceIdType.MESH
HALVES = (pl.ds(0, 256), pl.ds(256, 256))


class Place:
    def __init__(self):
        self.occ = lax.axis_index("occ")
        self.fit = lax.axis_index("fit")
        self.z, self.y = self.occ // 4, self.occ % 4
        self.x, self.low, self.core = self.fit // 4, (self.fit // 2) % 2, self.fit % 2

    def o(self, dz, dy):
        return ((self.z + dz + 4) % 4) * 4 + (self.y + dy + 4) % 4

    def f(self, dx, flip_low=0, flip_core=0):
        low = self.low if not flip_low else 1 - self.low
        core = self.core if not flip_core else 1 - self.core
        return ((self.x + dx + 4) % 4) * 4 + low * 2 + core


def entry_barrier(peers):
    barrier = pltpu.get_barrier_semaphore()
    for occ, fit in peers:
        pl.semaphore_signal(barrier, inc=1, device_id={"occ": occ, "fit": fit}, device_id_type=MESH)
    pl.semaphore_wait(barrier, len(peers))


def fit_kernel(fit_ref, int_ref, out_ref, acc, fb, ib, fsend, frecv, isend, irecv):
    at = Place()
    me = (at.occ, at.fit)
    entry_barrier(
        [(at.o(dz, dy), at.fit) for dz, dy in ((1, 0), (-1, 0), (0, 1), (0, -1))]
        + [(at.occ, at.f(1)), (at.occ, at.f(-1)), (at.occ, at.f(0, 1)), (at.occ, at.f(0, 0, 1))]
    )
    started = []

    def send(buf, recv, sends, src, slot, half, occ, fit):
        at_half = () if half is None else (HALVES[half],)
        sem = sends.at[len(started)]
        copy = pltpu.make_async_remote_copy(
            src_ref=src.at[at_half] if half is not None else src,
            dst_ref=buf.at[(slot,) + at_half],
            send_sem=sem,
            recv_sem=recv.at[slot, 0 if half is None else half],
            device_id={"occ": occ, "fit": fit},
            device_id_type=MESH,
        )
        copy.start()
        started.append(copy)

    def arrived(buf, recv, slot, half):
        part = buf.at[slot] if half is None else buf.at[slot, HALVES[half]]
        pltpu.make_async_remote_copy(
            src_ref=part,
            dst_ref=part,
            send_sem=fsend.at[0],
            recv_sem=recv.at[slot, 0 if half is None else half],
            device_id={"occ": me[0], "fit": me[1]},
            device_id_type=MESH,
        ).wait_recv()

    def fsnd(src, slot, half, dz, dy):
        send(fb, frecv, fsend, src, slot, half, at.o(dz, dy), at.fit)

    def isnd(src, slot, half, fit):
        send(ib, irecv, fsend, src, slot, half, at.occ, fit)

    def f_got(dz, dy):
        slot = at.o(dz, dy)
        if dz == 2 and dy == 0 or dy == 2:
            arrived(fb, frecv, slot, 0)
            arrived(fb, frecv, slot, 1)
        else:
            arrived(fb, frecv, slot, None)
        return slot

    def i_got(dx, flip_low):
        slot = at.f(dx, flip_low)
        if dx == 2:
            arrived(ib, irecv, slot, 0)
            arrived(ib, irecv, slot, 1)
        else:
            arrived(ib, irecv, slot, None)
        return slot

    def f_spread(dz):
        slot = at.o(dz, 0)
        src = fit_ref if dz == 0 else fb.at[slot]
        fsnd(src, slot, None, 0, 1)
        fsnd(src, slot, None, 0, -1)

    def f_relay_y(dz):
        slot = f_got(dz, 1)
        fsnd(fb.at[slot], slot, 0, 0, -1)
        slot = f_got(dz, -1)
        fsnd(fb.at[slot], slot, 1, 0, 1)

    def to_core(src, slot):
        isnd(src, slot, None, at.f(0, 0, 1))

    def i_spread(flip_low):
        slot = at.f(0, flip_low)
        src = ib.at[slot] if flip_low else int_ref
        isnd(src, slot, None, at.f(1))
        isnd(src, slot, None, at.f(-1))

    def i_relay(flip_low):
        slot = i_got(1, flip_low)
        isnd(ib.at[slot], slot, 0, at.f(-1))
        to_core(ib.at[slot], slot)
        slot = i_got(-1, flip_low)
        isnd(ib.at[slot], slot, 1, at.f(1))
        to_core(ib.at[slot], slot)

    def multiply(dy):
        for dz in (0, 1, -1, 2):
            if dy == 2:
                f_got(dz, 2)

        def one(k, carry):
            slot = at.o(k, dy)
            acc[...] += jnp.dot(fb[slot], ib[slot], preferred_element_type=jnp.float32)
            return carry

        lax.fori_loop(0, 4, one, 0)

    fsnd(fit_ref, at.occ, None, 1, 0)
    fsnd(fit_ref, at.occ, None, -1, 0)
    f_spread(0)
    i_spread(0)
    to_core(int_ref, at.fit)
    fb[at.occ] = fit_ref[...]
    ib[at.fit] = int_ref[...]
    acc[...] = jnp.zeros_like(acc)

    f_relay_y(0)
    i_relay(0)
    slot = i_got(2, 0)
    to_core(ib.at[slot], slot)
    slot = f_got(1, 0)
    fsnd(fb.at[slot], slot, 0, -1, 0)
    f_spread(1)
    slot = f_got(-1, 0)
    fsnd(fb.at[slot], slot, 1, 1, 0)
    f_spread(-1)
    isnd(int_ref, at.fit, None, at.f(0, 1))
    f_got(2, 0)
    f_spread(2)
    slot = i_got(0, 1)
    i_spread(1)
    to_core(ib.at[slot], slot)
    f_relay_y(1)
    i_relay(1)
    f_relay_y(-1)
    slot = i_got(2, 1)
    to_core(ib.at[slot], slot)
    f_relay_y(2)
    for flip_low in (0, 1):
        for dx in (0, 1, -1, 2):
            arrived(ib, irecv, at.f(dx, flip_low, 1), None)
    multiply(0)
    multiply(1)
    multiply(3)
    multiply(2)
    hi = acc[...].astype(jnp.bfloat16)
    out_ref[0] = hi
    out_ref[1] = (acc[...] - hi.astype(jnp.float32)).astype(jnp.bfloat16)
    for copy in started:
        copy.wait_send()


def fitted_of(fitting, integrals):
    sends = 37
    return pl.pallas_call(
        fit_kernel,
        out_shape=jax.ShapeDtypeStruct((2, 512, 512), jnp.bfloat16),
        in_specs=[pl.BlockSpec(memory_space=pltpu.VMEM)] * 2,
        out_specs=pl.BlockSpec(memory_space=pltpu.VMEM),
        scratch_shapes=[
            pltpu.VMEM((512, 512), jnp.float32),
            pltpu.VMEM((16, 512, 512), jnp.bfloat16),
            pltpu.VMEM((16, 512, 512), jnp.bfloat16),
            pltpu.SemaphoreType.DMA((sends,)),
            pltpu.SemaphoreType.DMA((16, 2)),
            pltpu.SemaphoreType.DMA((1,)),
            pltpu.SemaphoreType.DMA((16, 2)),
        ],
        compiler_params=pltpu.CompilerParams(
            collective_id=0, has_side_effects=True, vmem_limit_bytes=40 * 1024 * 1024
        ),
    )(fitting, integrals)


ORDER = (0, 4, 1, 3, 2, 5)
SLOT = {d: k for k, d in enumerate(ORDER)}
SPARE = 6
CHUNKS = 4
ROUTES = (
    (0, SLOT[4], -1, 0),
    (0, SLOT[1], 0, -1),
    (0, SLOT[3], 0, 1),
    (SLOT[1], SLOT[2], 0, -1),
    (SLOT[1], SLOT[5], -1, 0),
    (SLOT[4], SLOT[3], 0, 1),
    (SLOT[4], SLOT[5], 0, -1),
    (SLOT[4], SLOT[1], 0, -1),
    (SLOT[4], SPARE, -1, 0),
    (SLOT[3], SLOT[2], 0, 1),
    (SLOT[2], SLOT[5], 0, 1),
    (SPARE, SLOT[5], 0, -1),
)


def takes(route, y, c):
    return (
        True,
        y > 0,
        y == 3,
        y == 1,
        (y == 3) & (c < 2),
        y < 3,
        y >= 2,
        y == 0,
        (y == 0) & (c >= 2),
        y < 3,
        y == 3,
        (y == 0) & (c >= 2),
    )[route]


def dot_nt(a, b):
    return lax.dot_general(a, b, (((1,), (1,)), ((), ())), preferred_element_type=jnp.float32)


def dot_nn(a, b):
    return jnp.dot(a, b, preferred_element_type=jnp.float32)


def pair_kernel(
    own_ref, occ_ref, vrow_ref, vcol_ref, out_ref, en_ref,
    pt, spare, ownt, pbo, hb, cb, xb, qb, zb, am, eb,
    rs, rr, es, er, cs, cr, xs, xr, zs, zr, azs, azr, axs, axr, acs, acr,
):
    at = Place()
    y = at.y
    core_peer, low_peer = at.f(0, 0, 1), at.f(0, 1)
    x_peers = (at.f(1), at.f(-1), at.f(2))
    ahead = [(at.occ + d) % 16 for d in range(1, 6)]
    behind = [(at.occ + 16 - d) % 16 for d in range(1, 6)]
    entry_barrier(
        [(o, at.fit) for o in ahead + behind]
        + [(at.occ, f) for f in x_peers + (core_peer, low_peer)]
    )

    def remote(src, dst, ssem, rsem, occ, fit):
        return pltpu.make_async_remote_copy(
            src_ref=src, dst_ref=dst, send_sem=ssem, recv_sem=rsem,
            device_id={"occ": occ, "fit": fit}, device_id_type=MESH,
        )

    def rows(c):
        return pl.ds(pl.multiple_of(c * 128, 128), 128)

    def place(slot, c):
        if slot == SPARE:
            return spare.at[:, pl.ds(pl.multiple_of((c - 2) * 128, 128), 128)]
        return pt.at[slot, :, rows(c)]

    def route(n, c):
        src, dst, dz, dy = ROUTES[n]
        return remote(
            own_ref.at[:, rows(c)] if src == 0 else place(src, c),
            place(dst, c), rs.at[n, c], rr.at[dst, c], at.o(dz, dy), at.fit,
        )

    def send_on(slot, c):
        for n in range(len(ROUTES)):
            if ROUTES[n][0] == slot:
                pl.when(takes(n, y, c))(lambda n=n: route(n, c).start())

    def got(slot, c):
        part = place(slot, c)
        remote(part, part, rs.at[0, 0], rr.at[slot, c], at.occ, at.fit).wait_recv()

    def energy_copy(d):
        k = SLOT[d]
        return remote(occ_ref, eb.at[k], es.at[k], er.at[k], behind[d - 1], at.fit)

    mine = pl.ds(pl.multiple_of(at.core * 256, 256), 256)
    other = pl.ds(pl.multiple_of((1 - at.core) * 256, 256), 256)

    def quarter(x):
        return pl.ds(pl.multiple_of(x * 64, 64), 64)

    def core_copy(k):
        return remote(pbo.at[k], cb.at[k], cs.at[k], cr.at[k], at.occ, core_peer)

    def x_copy(k, n):
        to = (at.x + (1, 3, 2)[n]) % 4
        return remote(hb.at[k, quarter(to)], xb.at[k, n], xs.at[k, n], xr.at[k, n], at.occ, x_peers[n])

    def z_copy(k):
        half = pl.ds(pl.multiple_of((1 - at.low) * 32, 32), 32)
        return remote(qb.at[k, half], zb.at[k], zs.at[k], zr.at[k], at.occ, low_peer)

    def block(x, core):
        return pl.ds(pl.multiple_of(core * 256 + x * 64, 64), 64)

    own_rows = pl.ds(pl.multiple_of(at.core * 256 + at.x * 64 + at.low * 32, 32), 32)

    def az_copy(k):
        part = am.at[k, :, own_rows]
        return remote(part, part, azs.at[k], azr.at[k], at.occ, low_peer)

    def ax_copy(k, n):
        part = am.at[k, :, block(at.x, at.core)]
        return remote(part, part, axs.at[k, n], axr.at[k, n], at.occ, x_peers[n])

    def ac_copy(k, n):
        part = am.at[k, :, block((at.x + n) % 4, at.core)]
        return remote(part, part, acs.at[k, n], acr.at[k, n], at.occ, core_peer)

    def c1(k):
        @pl.when(k == 5)
        def _():
            for c in range(CHUNKS):
                got(SLOT[5], c)

        hi, lo = pt[k, 0], pt[k, 1]

        def part(where):
            return (
                dot_nn(ownt[0, where], hi) + dot_nn(ownt[0, where], lo) + dot_nn(ownt[1, where], hi)
            )

        pbo[k] = part(other)
        core_copy(k).start()
        hb[k] = part(mine)

    def c2(k):
        core_copy(k).wait_recv()
        hb[k] += cb[k]
        for n in range(3):
            x_copy(k, n).start()

    def c3(k):
        for n in range(3):
            x_copy(k, n).wait_recv()
        qb[k] = (hb[k, quarter(at.x)] + xb[k, 0]) + (xb[k, 1] + xb[k, 2])
        z_copy(k).start()

    def c4(k):
        z_copy(k).wait_recv()
        summed = qb[k, pl.ds(pl.multiple_of(at.low * 32, 32), 32)] + zb[k]
        energy = occ_ref[0:1, 0:1] + eb[k, 0:1, 0:1]
        denom = energy - vcol_ref[own_rows] - vrow_ref[...]
        amplitude = summed / denom
        hi = amplitude.astype(jnp.bfloat16)
        am[k, 0, own_rows] = hi
        am[k, 1, own_rows] = (amplitude - hi.astype(jnp.float32)).astype(jnp.bfloat16)
        az_copy(k).start()

    def c5(k):
        az_copy(k).wait_recv()
        for n in range(3):
            ax_copy(k, n).start()
        ac_copy(k, 0).start()

    def c6(k):
        for n in range(3):
            ax_copy(k, n).wait_recv()
            ac_copy(k, (3, 1, 2)[n]).start()

    def c7(k):
        for n in range(4):
            ac_copy(k, n).wait_recv()
        hi, lo = pt[k, 0], pt[k, 1]
        out_ref[...] += dot_nt(hi, am[k, 0]) + dot_nt(hi, am[k, 1]) + dot_nt(lo, am[k, 0])
        energy = occ_ref[0:1, 0:1] + eb[k, 0:1, 0:1]
        total = jnp.zeros((1, 1), jnp.float32)
        for r in range(4):
            band = pl.ds(r * 128, 128)
            a = am[k, 0, band].astype(jnp.float32) + am[k, 1, band].astype(jnp.float32)
            b = am[k, 0, :, band].astype(jnp.float32) + am[k, 1, :, band].astype(jnp.float32)
            denom = energy - vcol_ref[band] - vrow_ref[...]
            total += jnp.sum(a * denom * (2.0 * a - b.T), axis=(0, 1), keepdims=True)
        line = lax.broadcasted_iota(jnp.int32, en_ref.shape, 0)
        en_ref[...] += jnp.where(line == k, total, 0.0)

    for d in range(1, 6):
        energy_copy(d).start()
    for c in range(CHUNKS):
        send_on(0, c)
    pt[0] = own_ref[...]
    eb[0] = occ_ref[...]
    ownt[0] = own_ref[0].astype(jnp.float32).T.astype(jnp.bfloat16)
    ownt[1] = own_ref[1].astype(jnp.float32).T.astype(jnp.bfloat16)
    out_ref[...] = jnp.zeros_like(out_ref)
    en_ref[...] = jnp.zeros_like(en_ref)
    for d in range(1, 6):
        energy_copy(d).wait_recv()

    def step(r, carry):
        for slot, first in ((SLOT[4], 0), (SLOT[1], 0), (SLOT[3], 1), (SLOT[2], 2)):
            c = r - first

            @pl.when((c >= 0) & (c < CHUNKS))
            def _():
                got(slot, c)
                send_on(slot, c)

        c = r - 3

        @pl.when((c >= 2) & (c < CHUNKS) & (y == 0))
        def _():
            got(SPARE, c)
            send_on(SPARE, c)

        for j, stage in ((1, c2), (2, c3), (3, c4), (4, c5), (5, c6), (0, c1), (6, c7)):
            turn = r - j

            @pl.when((turn == 0) | ((turn >= 4) & (turn <= 8)))
            def _():
                stage(jnp.where(turn == 0, 0, turn - 3))

        return carry

    lax.fori_loop(0, 15, step, 0)

    for n in range(len(ROUTES)):
        for c in range(CHUNKS):
            pl.when(takes(n, y, c))(lambda n=n, c=c: route(n, c).wait_send())
    for d in range(1, 6):
        energy_copy(d).wait_send()

    def finish(k, carry):
        core_copy(k).wait_send()
        z_copy(k).wait_send()
        az_copy(k).wait_send()
        for n in range(3):
            x_copy(k, n).wait_send()
            ax_copy(k, n).wait_send()
        for n in range(4):
            ac_copy(k, n).wait_send()
        return carry

    lax.fori_loop(0, 6, finish, 0)


def pairs_of(fitted, occ_tile, vir_row, vir_col):
    f32, bf16 = jnp.float32, jnp.bfloat16
    dma = pltpu.SemaphoreType.DMA
    return pl.pallas_call(
        pair_kernel,
        out_shape=(
            jax.ShapeDtypeStruct((512, 512), f32),
            jax.ShapeDtypeStruct((8, 128), f32),
        ),
        in_specs=[pl.BlockSpec(memory_space=pltpu.VMEM)] * 4,
        out_specs=[pl.BlockSpec(memory_space=pltpu.VMEM)] * 2,
        scratch_shapes=[
            pltpu.VMEM((6, 2, 512, 512), bf16),
            pltpu.VMEM((2, 256, 512), bf16),
            pltpu.VMEM((2, 512, 512), bf16),
            pltpu.VMEM((6, 256, 512), f32),
            pltpu.VMEM((6, 256, 512), f32),
            pltpu.VMEM((6, 256, 512), f32),
            pltpu.VMEM((6, 3, 64, 512), f32),
            pltpu.VMEM((6, 64, 512), f32),
            pltpu.VMEM((6, 32, 512), f32),
            pltpu.VMEM((6, 2, 512, 512), bf16),
            pltpu.VMEM((6, 8, 128), f32),
            dma((len(ROUTES), CHUNKS)), dma((7, CHUNKS)),
            dma((6,)), dma((6,)),
            dma((6,)), dma((6,)),
            dma((6, 3)), dma((6, 3)),
            dma((6,)), dma((6,)),
            dma((6,)), dma((6,)),
            dma((6, 3)), dma((6, 3)),
            dma((6, 4)), dma((6, 4)),
        ],
        compiler_params=pltpu.CompilerParams(
            collective_id=1, has_side_effects=True, vmem_limit_bytes=56 * 1024 * 1024
        ),
    )(fitted, occ_tile, vir_row, vir_col)


def body(integrals, fitting, occ_energy, vir_energy):
    nvir = integrals.shape[2]
    fitted = fitted_of(fitting, integrals[:, 0, :])
    occ_tile = jnp.broadcast_to(occ_energy[:, None], (8, 128))
    density, energies = pairs_of(fitted, occ_tile, vir_energy[None, :], vir_energy[:, None])
    pair_energy = jnp.stack([energies[SLOT[d], 0] for d in range(STOPS)])[None, :] / (nvir * nvir)
    return (density[:, None, :], pair_energy)


def solution(mesh):
    placed = (P("fit", "occ", None), P("fit", "occ"), P("occ"), P())
    return jax.shard_map(
        body,
        mesh=mesh,
        in_specs=placed,
        out_specs=(P("fit", "occ", None), P("occ", None)),
        check_vma=False,
    )
```

```python
import jax
import jax.numpy as jnp
from jax import lax
from jax.experimental import pallas as pl
from jax.experimental.pallas import tpu as pltpu
from jax.sharding import PartitionSpec as P

STOPS = 6
MESH = pl.DeviceIdType.MESH


class Place:
    def __init__(self):
        self.occ = lax.axis_index("occ")
        self.fit = lax.axis_index("fit")
        self.z, self.y = self.occ // 4, self.occ % 4
        self.x, self.low, self.core = self.fit // 4, (self.fit // 2) % 2, self.fit % 2

    def o(self, dz, dy):
        return ((self.z + dz + 4) % 4) * 4 + (self.y + dy + 4) % 4

    def f(self, dx, flip_low=0, flip_core=0):
        low = self.low if not flip_low else 1 - self.low
        core = self.core if not flip_core else 1 - self.core
        return ((self.x + dx + 4) % 4) * 4 + low * 2 + core


def entry_barrier(peers):
    barrier = pltpu.get_barrier_semaphore()
    for occ, fit in peers:
        pl.semaphore_signal(barrier, inc=1, device_id={"occ": occ, "fit": fit}, device_id_type=MESH)
    pl.semaphore_wait(barrier, len(peers))


ORDER = (0, 4, 1, 3, 2, 5)
SLOT = {d: k for k, d in enumerate(ORDER)}
VIA, NEXT = 6, 7
CHUNKS = 4
ROUTES = (
    (0, SLOT[4], -1, 0),
    (0, SLOT[1], 0, -1),
    (0, SLOT[3], 0, 1),
    (0, VIA, 0, -1),
    (0, VIA, 1, 0),
    (SLOT[1], SLOT[2], 0, -1),
    (SLOT[4], SLOT[1], 0, -1),
    (SLOT[4], SLOT[3], 0, 1),
    (SLOT[4], SLOT[5], 0, -1),
    (SLOT[3], SLOT[2], 0, 1),
    (SLOT[2], SLOT[5], 0, 1),
    (VIA, NEXT, 1, 0),
    (NEXT, SLOT[5], 1, 0),
    (NEXT, SLOT[5], 0, -1),
)
HOPS = (
    (0, 0, None, "low"),
    (0, 0, None, 1),
    (0, 0, None, -1),
    (0, 0, None, "core"),
    (0, 1, None, 1),
    (0, 1, None, -1),
    (0, 1, None, "core"),
    (1, 0, 0, -1),
    (1, 0, None, "core"),
    (-1, 0, 1, 1),
    (-1, 0, None, "core"),
    (1, 1, 0, -1),
    (1, 1, None, "core"),
    (-1, 1, 1, 1),
    (-1, 1, None, "core"),
    (2, 0, None, "core"),
    (2, 1, None, "core"),
)


def carries(y, c):
    return ((y == 3) & (c < 2)) | ((y == 0) & (c >= 2))


def takes(route, y, c):
    return (
        True,
        y > 0,
        y == 3,
        (y == 0) & (c < 2),
        (y == 0) & (c >= 2),
        y == 1,
        y == 0,
        y < 3,
        y >= 2,
        y < 3,
        y == 3,
        carries(y, c),
        (y == 3) & (c < 2),
        (y == 0) & (c >= 2),
    )[route]


def dot_nt(a, b):
    return lax.dot_general(a, b, (((1,), (1,)), ((), ())), preferred_element_type=jnp.float32)


def dot_nn(a, b):
    return jnp.dot(a, b, preferred_element_type=jnp.float32)


def kernel(
    fit_ref, int_ref, occ_ref, vir_ref, out_ref, en_ref,
    fb, ib, acc, pt, spare, ownt, pbo, hb, cb, xb, qb, zb, am, eb, vcol,
    fs, fr, js, jr, rs, rr, es, er, cs, cr, xs, xr, zs, zr, azs, azr, axs, axr, acs, acr,
):
    at = Place()
    y = at.y
    core_peer, low_peer = at.f(0, 0, 1), at.f(0, 1)
    x_peers = (at.f(1), at.f(-1), at.f(2))
    ahead = [(at.occ + d) % 16 for d in range(1, 6)]
    behind = [(at.occ + 16 - d) % 16 for d in range(1, 6)]
    entry_barrier(
        [(o, at.fit) for o in ahead + behind]
        + [(at.occ, f) for f in x_peers + (core_peer, low_peer)]
    )

    def remote(src, dst, ssem, rsem, occ, fit):
        return pltpu.make_async_remote_copy(
            src_ref=src, dst_ref=dst, send_sem=ssem, recv_sem=rsem,
            device_id={"occ": occ, "fit": fit}, device_id_type=MESH,
        )

    def rows(c):
        return pl.ds(pl.multiple_of(c * 128, 128), 128)

    def rows_of(c, half):
        if half is None:
            return rows(c)
        return pl.ds(pl.multiple_of(c * 128 + half * 64, 64), 64)

    def f_copy(n, c):
        if n < 2:
            slot, half, own, to = at.occ, None, True, at.o((1, -1)[n], 0)
        elif n < 4:
            slot, half, own, to = at.o((1, -1)[n - 2], 0), n - 2, False, at.o((-1, 1)[n - 2], 0)
        elif n < 12:
            dz, up = (n - 4) // 2, (n - 4) % 2
            slot, half, own, to = at.o(dz, 0), None, dz == 0, at.o(0, (1, -1)[up])
        else:
            dz, up = (n - 12) // 2, (n - 12) % 2
            slot, half, own, to = at.o(dz, (1, -1)[up]), up, False, at.o(0, (-1, 1)[up])
        where = rows_of(c, half)
        src = fit_ref.at[where] if own else fb.at[slot, where]
        return remote(src, fb.at[slot, where], fs.at[n, c], fr.at[slot, c, half or 0], to, at.fit)

    def f_got(dz, dy, c):
        slot = at.o(dz, dy)
        for half in ((0, 1) if dy == 2 or (dz == 2 and dy == 0) else (None,)):
            part = fb.at[slot, rows_of(c, half)]
            remote(part, part, fs.at[0, 0], fr.at[slot, c, half or 0], at.occ, at.fit).wait_recv()

    def f_spread(dz, c):
        f_copy(4 + 2 * dz, c).start()
        f_copy(5 + 2 * dz, c).start()

    def f_first(c):
        f_got(1, 0, c)
        f_copy(2, c).start()
        f_spread(1, c)
        f_got(3, 0, c)
        f_copy(3, c).start()
        f_spread(3, c)
        f_got(2, 0, c)
        f_spread(2, c)

    def f_second(c):
        for dz in (0, 1, 3, 2):
            f_got(dz, 1, c)
            f_copy(12 + 2 * dz, c).start()
            f_got(dz, 3, c)
            f_copy(13 + 2 * dz, c).start()

    def j_copy(n):
        dx, flip_low, half, to = HOPS[n]
        slot = at.f(dx, flip_low)
        where = pl.ds(0, 512) if half is None else pl.ds(half * 256, 256)
        src = int_ref.at[where] if (dx, flip_low) == (0, 0) else ib.at[slot, where]
        fit = {"low": low_peer, "core": core_peer, 1: at.f(1), -1: at.f(-1)}[to]
        return remote(src, ib.at[slot, where], js.at[n], jr.at[slot, half or 0], at.occ, fit)

    def j_send(*hops):
        for hop in hops:
            j_copy(HOPS.index(hop)).start()

    def j_got(slot, halves):
        for half in (0, 1) if halves else (None,):
            where = pl.ds(0, 512) if half is None else pl.ds(half * 256, 256)
            part = ib.at[slot, where]
            remote(part, part, js.at[0], jr.at[slot, half or 0], at.occ, at.fit).wait_recv()

    def j_relay(flip_low):
        for dx, half in ((1, 0), (-1, 1)):
            j_got(at.f(dx, flip_low), False)
            j_send((dx, flip_low, half, -dx), (dx, flip_low, None, "core"))

    def j_last(flip_low):
        j_got(at.f(2, flip_low), True)
        j_send((2, flip_low, None, "core"))

    def j_low():
        j_got(at.f(0, 1), False)
        j_send((0, 1, None, 1), (0, 1, None, -1), (0, 1, None, "core"))

    def j_core():
        for flip_low in (0, 1):
            for dx in (0, 1, -1, 2):
                j_got(at.f(dx, flip_low, 1), False)

    def place(slot, c):
        if slot >= VIA:
            return spare.at[slot - VIA, :, pl.ds(pl.multiple_of((c % 2) * 128, 128), 128)]
        return pt.at[slot, :, rows(c)]

    def route(n, c):
        src, dst, dz, dy = ROUTES[n]
        return remote(place(src, c), place(dst, c), rs.at[n, c], rr.at[dst, c], at.o(dz, dy), at.fit)

    def send_on(slot, c):
        for n in range(len(ROUTES)):
            if ROUTES[n][0] == slot:
                pl.when(takes(n, y, c))(lambda n=n: route(n, c).start())

    def got(slot, c):
        part = place(slot, c)
        remote(part, part, rs.at[0, 0], rr.at[slot, c], at.occ, at.fit).wait_recv()

    def energy_copy(d):
        k = SLOT[d]
        return remote(eb.at[0], eb.at[k], es.at[k], er.at[k], behind[d - 1], at.fit)

    def fit_chunk(c):
        def add(dy):
            def one(dz, carry):
                slot = at.o(dz, dy)
                acc[...] += dot_nn(fb[slot, rows(c)], ib[slot])
                return carry

            lax.fori_loop(0, 4, one, 0)

        acc[...] = jnp.zeros_like(acc)
        for dy in (0, 1, 3):
            add(dy)
        for dz in range(4):
            f_got(dz, 2, c)
        add(2)
        whole = acc[...]
        hi = whole.astype(jnp.bfloat16)
        low = whole - hi.astype(jnp.float32)
        pt[0, 0, rows(c)] = hi
        pt[0, 1, rows(c)] = low.astype(jnp.bfloat16)
        ownt[0, :, rows(c)] = hi.astype(jnp.float32).T.astype(jnp.bfloat16)
        ownt[1, :, rows(c)] = low.T.astype(jnp.bfloat16)
        send_on(0, c)

    mine = pl.ds(pl.multiple_of(at.core * 256, 256), 256)
    other = pl.ds(pl.multiple_of((1 - at.core) * 256, 256), 256)

    def quarter(x):
        return pl.ds(pl.multiple_of(x * 64, 64), 64)

    def core_copy(k):
        return remote(pbo.at[k], cb.at[k], cs.at[k], cr.at[k], at.occ, core_peer)

    def x_copy(k, n):
        to = (at.x + (1, 3, 2)[n]) % 4
        return remote(hb.at[k, quarter(to)], xb.at[k, n], xs.at[k, n], xr.at[k, n], at.occ, x_peers[n])

    def z_copy(k):
        half = pl.ds(pl.multiple_of((1 - at.low) * 32, 32), 32)
        return remote(qb.at[k, half], zb.at[k], zs.at[k], zr.at[k], at.occ, low_peer)

    def block(x, core):
        return pl.ds(pl.multiple_of(core * 256 + x * 64, 64), 64)

    own_rows = pl.ds(pl.multiple_of(at.core * 256 + at.x * 64 + at.low * 32, 32), 32)

    def az_copy(k):
        part = am.at[k, :, own_rows]
        return remote(part, part, azs.at[k], azr.at[k], at.occ, low_peer)

    def ax_copy(k, n):
        part = am.at[k, :, block(at.x, at.core)]
        return remote(part, part, axs.at[k, n], axr.at[k, n], at.occ, x_peers[n])

    def ac_copy(k, n):
        part = am.at[k, :, block((at.x + n) % 4, at.core)]
        return remote(part, part, acs.at[k, n], acr.at[k, n], at.occ, core_peer)

    def c1(k):
        @pl.when(k == 5)
        def _():
            for c in range(CHUNKS):
                got(SLOT[5], c)

        hi, lo = pt[k, 0], pt[k, 1]

        def part(where):
            return (
                dot_nn(ownt[0, where], hi) + dot_nn(ownt[0, where], lo) + dot_nn(ownt[1, where], hi)
            )

        pbo[k] = part(other)
        core_copy(k).start()
        hb[k] = part(mine)

    def c2(k):
        core_copy(k).wait_recv()
        hb[k] += cb[k]
        for n in range(3):
            x_copy(k, n).start()

    def c3(k):
        for n in range(3):
            x_copy(k, n).wait_recv()
        qb[k] = (hb[k, quarter(at.x)] + xb[k, 0]) + (xb[k, 1] + xb[k, 2])
        z_copy(k).start()

    def c4(k):
        z_copy(k).wait_recv()
        summed = qb[k, pl.ds(pl.multiple_of(at.low * 32, 32), 32)] + zb[k]
        energy = eb[0, 0:1, 0:1] + eb[k, 0:1, 0:1]
        denom = energy - vcol[own_rows, 0:1] - vir_ref[...]
        amplitude = summed / denom
        hi = amplitude.astype(jnp.bfloat16)
        am[k, 0, own_rows] = hi
        am[k, 1, own_rows] = (amplitude - hi.astype(jnp.float32)).astype(jnp.bfloat16)
        az_copy(k).start()

    def c5(k):
        az_copy(k).wait_recv()
        for n in range(3):
            ax_copy(k, n).start()
        ac_copy(k, 0).start()

    def c6(k):
        for n in range(3):
            ax_copy(k, n).wait_recv()
            ac_copy(k, (3, 1, 2)[n]).start()

    def c7(k):
        for n in range(4):
            ac_copy(k, n).wait_recv()
        hi, lo = pt[k, 0], pt[k, 1]
        out_ref[...] += dot_nt(hi, am[k, 0]) + dot_nt(hi, am[k, 1]) + dot_nt(lo, am[k, 0])
        energy = eb[0, 0:1, 0:1] + eb[k, 0:1, 0:1]
        total = jnp.zeros((1, 1), jnp.float32)
        for r in range(4):
            band = pl.ds(r * 128, 128)
            a = am[k, 0, band].astype(jnp.float32) + am[k, 1, band].astype(jnp.float32)
            b = am[k, 0, :, band].astype(jnp.float32) + am[k, 1, :, band].astype(jnp.float32)
            denom = energy - vcol[band, 0:1] - vir_ref[...]
            total += jnp.sum(a * denom * (2.0 * a - b.T), axis=(0, 1), keepdims=True)
        d = 0
        for place_of, distance in enumerate(ORDER):
            d += jnp.where(k == place_of, distance, 0)
        lane = lax.broadcasted_iota(jnp.int32, en_ref.shape, 1)
        en_ref[...] += jnp.where(lane == d, total / (512 * 512), 0.0)

    j_send((0, 0, None, "low"))
    for c in range(CHUNKS):
        f_copy(0, c).start()
        f_copy(1, c).start()
        if c < 2:
            f_spread(0, c)
    j_send((0, 0, None, 1), (0, 0, None, -1), (0, 0, None, "core"))
    fb[at.occ] = fit_ref[...]
    ib[at.fit] = int_ref[...]
    eb[0] = jnp.broadcast_to(occ_ref[...], (8, 128))
    out_ref[...] = jnp.zeros_like(out_ref)
    en_ref[...] = jnp.zeros_like(en_ref)
    vcol[...] = jnp.broadcast_to(vir_ref[...], (128, 512)).T
    for d in range(1, 6):
        energy_copy(d).start()

    def step(t, carry):
        @pl.when(t < CHUNKS)
        def _():
            f_first(t)

        @pl.when(t < 2)
        def _():
            f_spread(0, t + 2)

        @pl.when(t == 0)
        def _():
            j_relay(0)
            j_low()

        @pl.when((t >= 1) & (t <= CHUNKS))
        def _():
            f_second(t - 1)

        @pl.when(t == 1)
        def _():
            j_last(0)
            j_relay(1)

        @pl.when(t == 2)
        def _():
            j_last(1)
            j_core()
            fit_chunk(0)
            for d in range(1, 6):
                energy_copy(d).wait_recv()

        @pl.when((t >= 2) & (t <= CHUNKS))
        def _():
            fit_chunk(t - 1)

        for slot, first in ((SLOT[4], 3), (SLOT[1], 3), (SLOT[3], 4), (SLOT[2], 5)):
            c = t - first

            @pl.when((c >= 0) & (c < CHUNKS))
            def _():
                got(slot, c)
                send_on(slot, c)

        for slot, first in ((VIA, 3), (NEXT, 4)):
            c = t - first

            @pl.when((c >= 0) & (c < CHUNKS) & carries(y, c))
            def _():
                got(slot, c)
                send_on(slot, c)

        for j, stage in ((1, c2), (2, c3), (3, c4), (4, c5), (5, c6), (0, c1), (6, c7)):
            turn = t - 4 - j

            @pl.when((turn == 0) | ((turn >= 2) & (turn <= 6)))
            def _():
                stage(jnp.where(turn == 0, 0, turn - 1))

        return carry

    lax.fori_loop(0, 17, step, 0)

    for n in range(20):
        lax.fori_loop(0, CHUNKS, lambda c, _: (f_copy(n, c).wait_send(), _)[1], 0)
    for n in range(len(HOPS)):
        j_copy(n).wait_send()
    for n in range(len(ROUTES)):
        for c in range(CHUNKS):
            pl.when(takes(n, y, c))(lambda n=n, c=c: route(n, c).wait_send())
    for d in range(1, 6):
        energy_copy(d).wait_send()

    def finish(k, carry):
        core_copy(k).wait_send()
        z_copy(k).wait_send()
        az_copy(k).wait_send()
        for n in range(3):
            x_copy(k, n).wait_send()
            ax_copy(k, n).wait_send()
        for n in range(4):
            ac_copy(k, n).wait_send()
        return carry

    lax.fori_loop(0, 6, finish, 0)


def run(fitting, integrals, occ_energy, vir_energy):
    f32, bf16 = jnp.float32, jnp.bfloat16
    dma = pltpu.SemaphoreType.DMA
    return pl.pallas_call(
        kernel,
        out_shape=(
            jax.ShapeDtypeStruct((512, 512), f32),
            jax.ShapeDtypeStruct((8, 128), f32),
        ),
        in_specs=[pl.BlockSpec(memory_space=pltpu.VMEM)] * 4,
        out_specs=[pl.BlockSpec(memory_space=pltpu.VMEM)] * 2,
        scratch_shapes=[
            pltpu.VMEM((16, 512, 512), bf16),
            pltpu.VMEM((16, 512, 512), bf16),
            pltpu.VMEM((128, 512), f32),
            pltpu.VMEM((6, 2, 512, 512), bf16),
            pltpu.VMEM((2, 2, 256, 512), bf16),
            pltpu.VMEM((2, 512, 512), bf16),
            pltpu.VMEM((6, 256, 512), f32),
            pltpu.VMEM((6, 256, 512), f32),
            pltpu.VMEM((6, 256, 512), f32),
            pltpu.VMEM((6, 3, 64, 512), f32),
            pltpu.VMEM((6, 64, 512), f32),
            pltpu.VMEM((6, 32, 512), f32),
            pltpu.VMEM((6, 2, 512, 512), bf16),
            pltpu.VMEM((6, 8, 128), f32),
            pltpu.VMEM((512, 128), f32),
            dma((20, CHUNKS)), dma((16, CHUNKS, 2)),
            dma((17,)), dma((16, 2)),
            dma((len(ROUTES), CHUNKS)), dma((8, CHUNKS)),
            dma((6,)), dma((6,)),
            dma((6,)), dma((6,)),
            dma((6, 3)), dma((6, 3)),
            dma((6,)), dma((6,)),
            dma((6,)), dma((6,)),
            dma((6, 3)), dma((6, 3)),
            dma((6, 4)), dma((6, 4)),
        ],
        compiler_params=pltpu.CompilerParams(
            collective_id=0, has_side_effects=True, vmem_limit_bytes=60 * 1024 * 1024
        ),
    )(fitting, integrals, occ_energy, vir_energy)


def body(integrals, fitting, occ_energy, vir_energy):
    density, energies = run(fitting, integrals[:, 0, :], occ_energy[:, None], vir_energy[None, :])
    return (density[:, None, :], energies[0:1, 0:STOPS])


def solution(mesh):
    placed = (P("fit", "occ", None), P("fit", "occ"), P("occ"), P())
    return jax.shard_map(
        body,
        mesh=mesh,
        in_specs=placed,
        out_specs=(P("fit", "occ", None), P("occ", None)),
        check_vma=False,
    )
```

```python
import jax
import jax.numpy as jnp
from jax import lax
from jax.experimental import pallas as pl
from jax.experimental.pallas import tpu as pltpu
from jax.sharding import PartitionSpec as P

STOPS = 6
MESH = pl.DeviceIdType.MESH


class Place:
    def __init__(self):
        self.occ = lax.axis_index("occ")
        self.fit = lax.axis_index("fit")
        self.z, self.y = self.occ // 4, self.occ % 4
        self.x, self.low, self.core = self.fit // 4, (self.fit // 2) % 2, self.fit % 2

    def o(self, dz, dy):
        return ((self.z + dz + 4) % 4) * 4 + (self.y + dy + 4) % 4

    def f(self, dx, flip_low=0, flip_core=0):
        low = self.low if not flip_low else 1 - self.low
        core = self.core if not flip_core else 1 - self.core
        return ((self.x + dx + 4) % 4) * 4 + low * 2 + core


def entry_barrier(peers):
    barrier = pltpu.get_barrier_semaphore()
    for occ, fit in peers:
        pl.semaphore_signal(barrier, inc=1, device_id={"occ": occ, "fit": fit}, device_id_type=MESH)
    pl.semaphore_wait(barrier, len(peers))


ORDER = (0, 4, 1, 3, 2, 5)
SLOT = {d: k for k, d in enumerate(ORDER)}
VIA, NEXT = 6, 7
CHUNKS = 4
ROUTES = (
    (0, SLOT[4], -1, 0),
    (0, SLOT[1], 0, -1),
    (0, SLOT[3], 0, 1),
    (0, VIA, 0, -1),
    (0, VIA, 1, 0),
    (SLOT[1], SLOT[2], 0, -1),
    (SLOT[4], SLOT[1], 0, -1),
    (SLOT[4], SLOT[3], 0, 1),
    (SLOT[4], SLOT[5], 0, -1),
    (SLOT[3], SLOT[2], 0, 1),
    (SLOT[2], SLOT[5], 0, 1),
    (VIA, NEXT, 1, 0),
    (NEXT, SLOT[5], 1, 0),
    (NEXT, SLOT[5], 0, -1),
)
HOPS = tuple((0, 0, h, to) for h in (0, 1) for to in ("low", 1, -1)) + tuple(
    (0, 1, h, to) for h in (0, 1) for to in (1, -1)
) + ((0, 0, None, "core"), (0, 1, None, "core")) + tuple(
    hop
    for low in (0, 1)
    for hop in (
        (1, low, 0, -1),
        (-1, low, 1, 1),
        (1, low, None, "core"),
        (-1, low, None, "core"),
        (2, low, None, "core"),
    )
)
PLAN = (
    ("oz", 0), ("oy", 2), ("jl", 0), ("jl", 1), ("oz", 1), ("jo",), ("oy", 3), ("oz", 2), ("oy", 0),
    ("jr", 0, 0), ("a3", 0), ("a1", 0), ("oy", 1), ("b", 0, 3), ("b", 3, 0), ("b", 1, 0), ("oz", 3),
    ("jg", 0), ("b", 0, 0), ("a1", 1), ("jg", 1), ("a3", 1), ("a1", 3), ("jr", 0, 1), ("a3", 2),
    ("jt", 0), ("jr", 1, 0), ("jr", 1, 1), ("a2", 0), ("b", 1, 1), ("jt", 1), ("b", 0, 1),
    ("b", 2, 0), ("a1", 2), ("b", 3, 1), ("f1", 0), ("a2", 1), ("f2", 0), ("b", 3, 2), ("a2", 2),
    ("b", 2, 1), ("a3", 3), ("b", 0, 2), ("b", 1, 2), ("f1", 1), ("b", 2, 2), ("f2", 1), ("a2", 3),
    ("f1", 2), ("b", 1, 3), ("b", 3, 3), ("f2", 2), ("b", 2, 3), ("py", 0), ("g", 4, 0, 1),
    ("g", 4, 0, 0), ("f1", 3), ("py", 1), ("g", 4, 1, 1), ("f2", 3), ("g", 4, 0, 2), ("g", 4, 1, 0),
    ("c", 1, 0), ("py", 2), ("c", 2, 0), ("g", "V", 2, 0), ("g", 3, 0, 0), ("g", 3, 0, 1),
    ("g", 4, 2, 1), ("g", 3, 1, 1), ("g", 3, 0, 2), ("g", 3, 1, 2), ("g", 1, 0, 3), ("py", 3),
    ("g", "V", 0, 3), ("g", 4, 2, 3), ("c", 3, 0), ("c", 4, 0), ("g", 4, 2, 0), ("g", 4, 0, 3),
    ("g", 4, 1, 2), ("g", 1, 0, 0), ("g", 2, 0, 3), ("g", 3, 1, 0), ("g", 4, 2, 2), ("g", 4, 1, 3),
    ("g", 1, 1, 1), ("g", "V", 3, 0), ("g", 1, 0, 2), ("g", 1, 0, 1), ("g", 4, 3, 3), ("c", 5, 0),
    ("g", 1, 2, 2), ("g", 1, 1, 3), ("g", 4, 3, 0), ("g", "V", 1, 3), ("g", 1, 1, 2),
    ("g", 1, 3, 2), ("g", 4, 3, 1), ("g", 1, 1, 0), ("g", 4, 3, 2), ("g", 1, 2, 0), ("c", 1, 1),
    ("c", 2, 1), ("g", "N", 0, 3), ("g", 3, 1, 3), ("g", 1, 3, 0), ("g", 1, 3, 3), ("g", 3, 3, 0),
    ("g", 2, 1, 3), ("g", 3, 0, 3), ("g", 2, 0, 2), ("g", 1, 2, 1), ("g", 3, 2, 3), ("g", 3, 2, 2),
    ("g", 1, 2, 3), ("g", 1, 3, 1), ("g", 3, 2, 0), ("g", 3, 2, 1), ("g", 2, 1, 2), ("c", 1, 2),
    ("c", 2, 2), ("g", 3, 3, 1), ("g", 3, 3, 3), ("g", 3, 3, 2), ("c", 1, 3), ("c", 3, 1),
    ("c", 2, 3), ("g", 2, 0, 0), ("g", 2, 0, 1), ("g", 2, 1, 1), ("g", 2, 2, 3), ("c", 4, 1),
    ("c", 3, 2), ("g", 2, 1, 0), ("g", 2, 3, 1), ("c", 5, 1), ("g", "N", 1, 3), ("g", 2, 2, 0),
    ("g", "N", 3, 0), ("g", 2, 3, 2), ("c", 3, 3), ("g", 2, 2, 2), ("g", 2, 3, 0), ("g", 2, 3, 3),
    ("c", 6, 0), ("c", 4, 2), ("g", "N", 2, 0), ("g", 2, 2, 1), ("c", 1, 4), ("c", 2, 4),
    ("c", 4, 3), ("c", 5, 3), ("c", 3, 4), ("c", 1, 5), ("c", 2, 5), ("c", 5, 2), ("c", 6, 1),
    ("c", 6, 3), ("c", 7, 0), ("c", 4, 4), ("c", 7, 1), ("c", 3, 5), ("c", 5, 4), ("c", 6, 2),
    ("c", 4, 5), ("c", 7, 3), ("c", 5, 5), ("c", 6, 4), ("c", 7, 2), ("c", 7, 4), ("c", 6, 5),
    ("c", 7, 5),
)


def carries(y, c):
    return ((y == 3) & (c < 2)) | ((y == 0) & (c >= 2))


def takes(route, y, c):
    return (
        True,
        y > 0,
        y == 3,
        (y == 0) & (c < 2),
        (y == 0) & (c >= 2),
        y == 1,
        y == 0,
        y < 3,
        y >= 2,
        y < 3,
        y == 3,
        carries(y, c),
        (y == 3) & (c < 2),
        (y == 0) & (c >= 2),
    )[route]


def dot_nt(a, b):
    return lax.dot_general(a, b, (((1,), (1,)), ((), ())), preferred_element_type=jnp.float32)


def dot_nn(a, b):
    return jnp.dot(a, b, preferred_element_type=jnp.float32)


def kernel(
    fit_ref, int_ref, occ_ref, vir_ref, out_ref, en_ref,
    fb, ib, acc, pt, spare, ownt, pbo, hb, cb, xb, qb, zb, am, eb, vcol,
    fs, fr, js, jr, rs, rr, es, er, cs, cr, xs, xr, zs, zr, azs, azr, axs, axr, acs, acr,
):
    at = Place()
    y = at.y
    core_peer, low_peer = at.f(0, 0, 1), at.f(0, 1)
    x_peers = (at.f(1), at.f(-1), at.f(2))
    ahead = [(at.occ + d) % 16 for d in range(1, 6)]
    behind = [(at.occ + 16 - d) % 16 for d in range(1, 6)]
    entry_barrier(
        [(o, at.fit) for o in ahead + behind]
        + [(at.occ, f) for f in x_peers + (core_peer, low_peer)]
    )

    def remote(src, dst, ssem, rsem, occ, fit):
        return pltpu.make_async_remote_copy(
            src_ref=src, dst_ref=dst, send_sem=ssem, recv_sem=rsem,
            device_id={"occ": occ, "fit": fit}, device_id_type=MESH,
        )

    def rows(c):
        return pl.ds(pl.multiple_of(c * 128, 128), 128)

    def rows_of(c, half):
        if half is None:
            return rows(c)
        return pl.ds(pl.multiple_of(c * 128 + half * 64, 64), 64)

    def f_copy(n, c):
        if n < 2:
            slot, half, own, to = at.occ, None, True, at.o((1, -1)[n], 0)
        elif n < 4:
            slot, half, own, to = at.o((1, -1)[n - 2], 0), n - 2, False, at.o((-1, 1)[n - 2], 0)
        elif n < 12:
            dz, up = (n - 4) // 2, (n - 4) % 2
            slot, half, own, to = at.o(dz, 0), None, dz == 0, at.o(0, (1, -1)[up])
        else:
            dz, up = (n - 12) // 2, (n - 12) % 2
            slot, half, own, to = at.o(dz, (1, -1)[up]), up, False, at.o(0, (-1, 1)[up])
        where = rows_of(c, half)
        src = fit_ref.at[where] if own else fb.at[slot, where]
        return remote(src, fb.at[slot, where], fs.at[n, c], fr.at[slot, c, half or 0], to, at.fit)

    def f_got(dz, dy, c):
        slot = at.o(dz, dy)
        for half in ((0, 1) if dy == 2 or (dz == 2 and dy == 0) else (None,)):
            part = fb.at[slot, rows_of(c, half)]
            remote(part, part, fs.at[0, 0], fr.at[slot, c, half or 0], at.occ, at.fit).wait_recv()

    def f_spread(dz, c):
        f_copy(4 + 2 * dz, c).start()
        f_copy(5 + 2 * dz, c).start()

    def f_near(dz, c):
        f_got(dz, 0, c)
        f_copy(2 if dz == 1 else 3, c).start()
        f_spread(dz, c)

    def f_far(c):
        f_got(2, 0, c)
        f_spread(2, c)

    def f_side(dz, c):
        f_got(dz, 1, c)
        f_got(dz, 3, c)
        f_copy(12 + 2 * dz, c).start()
        f_copy(13 + 2 * dz, c).start()

    def j_copy(n):
        dx, flip_low, half, to = HOPS[n]
        slot = at.f(dx, flip_low)
        where = pl.ds(0, 512) if half is None else pl.ds(half * 256, 256)
        src = int_ref.at[where] if (dx, flip_low) == (0, 0) else ib.at[slot, where]
        fit = {"low": low_peer, "core": core_peer, 1: at.f(1), -1: at.f(-1)}[to]
        return remote(src, ib.at[slot, where], js.at[n], jr.at[slot, half or 0], at.occ, fit)

    def j_send(*hops):
        for hop in hops:
            j_copy(HOPS.index(hop)).start()

    def j_got(slot, half):
        where = pl.ds(0, 512) if half is None else pl.ds(half * 256, 256)
        part = ib.at[slot, where]
        remote(part, part, js.at[0], jr.at[slot, half or 0], at.occ, at.fit).wait_recv()

    def j_own():
        for h in (0, 1):
            j_send((0, 0, h, -1), (0, 0, 1 - h, 1))
        j_send((0, 0, None, "core"))

    def j_low(h):
        j_got(at.f(0, 1), h)
        j_send((0, 1, h, -1), (0, 1, h, 1))
        if h == 1:
            j_send((0, 1, None, "core"))

    def j_relay(second, low):
        j_got(at.f(1, low), second)
        j_got(at.f(-1, low), 1 - second)
        if second:
            j_send((1, low, None, "core"), (-1, low, None, "core"))
        else:
            j_send((1, low, 0, -1), (-1, low, 1, 1))

    def j_last(low):
        j_got(at.f(2, low), 0)
        j_got(at.f(2, low), 1)
        j_send((2, low, None, "core"))

    def j_core():
        for low in (0, 1):
            for dx in (0, 1, -1, 2):
                j_got(at.f(dx, low, 1), None)

    def place(slot, c):
        if slot >= VIA:
            return spare.at[slot - VIA, :, pl.ds(pl.multiple_of((c % 2) * 128, 128), 128)]
        return pt.at[slot, :, rows(c)]

    def route(n, c):
        src, dst, dz, dy = ROUTES[n]
        return remote(place(src, c), place(dst, c), rs.at[n, c], rr.at[dst, c], at.o(dz, dy), at.fit)

    def send_on(slot, c, over_z=None):
        for n, (source, _, dz, _) in enumerate(ROUTES):
            if source == slot and over_z in (None, dz != 0):
                pl.when(takes(n, y, c))(lambda n=n: route(n, c).start())

    def got(slot, c):
        part = place(slot, c)
        remote(part, part, rs.at[0, 0], rr.at[slot, c], at.occ, at.fit).wait_recv()

    def energy_copy(d):
        k = SLOT[d]
        return remote(eb.at[0], eb.at[k], es.at[k], er.at[k], behind[d - 1], at.fit)

    def add(dy, c):
        def one(dz, carry):
            slot = at.o(dz, dy)
            acc[...] += dot_nn(fb[slot, rows(c)], ib[slot])
            return carry

        lax.fori_loop(0, 4, one, 0)

    def fit_most(c):
        if c == 0:
            j_core()
        acc[...] = jnp.zeros_like(acc)
        for dy in (0, 1, 3):
            add(dy, c)

    def fit_rest(c):
        for dz in range(4):
            f_got(dz, 2, c)
        add(2, c)
        whole = acc[...]
        hi = whole.astype(jnp.bfloat16)
        low = whole - hi.astype(jnp.float32)
        pt[0, 0, rows(c)] = hi
        pt[0, 1, rows(c)] = low.astype(jnp.bfloat16)
        ownt[0, :, rows(c)] = hi.astype(jnp.float32).T.astype(jnp.bfloat16)
        ownt[1, :, rows(c)] = low.T.astype(jnp.bfloat16)
        send_on(0, c, True)

    mine = pl.ds(pl.multiple_of(at.core * 256, 256), 256)
    other = pl.ds(pl.multiple_of((1 - at.core) * 256, 256), 256)

    def quarter(x):
        return pl.ds(pl.multiple_of(x * 64, 64), 64)

    def core_copy(k):
        return remote(pbo.at[k], cb.at[k], cs.at[k], cr.at[k], at.occ, core_peer)

    def x_copy(k, n):
        to = (at.x + (1, 3, 2)[n]) % 4
        return remote(hb.at[k, quarter(to)], xb.at[k, n], xs.at[k, n], xr.at[k, n], at.occ, x_peers[n])

    def z_copy(k):
        half = pl.ds(pl.multiple_of((1 - at.low) * 32, 32), 32)
        return remote(qb.at[k, half], zb.at[k], zs.at[k], zr.at[k], at.occ, low_peer)

    def block(x, core):
        return pl.ds(pl.multiple_of(core * 256 + x * 64, 64), 64)

    own_rows = pl.ds(pl.multiple_of(at.core * 256 + at.x * 64 + at.low * 32, 32), 32)

    def az_copy(k):
        part = am.at[k, :, own_rows]
        return remote(part, part, azs.at[k], azr.at[k], at.occ, low_peer)

    def ax_copy(k, n):
        part = am.at[k, :, block(at.x, at.core)]
        return remote(part, part, axs.at[k, n], axr.at[k, n], at.occ, x_peers[n])

    def ac_copy(k, n):
        part = am.at[k, :, block((at.x + n) % 4, at.core)]
        return remote(part, part, acs.at[k, n], acr.at[k, n], at.occ, core_peer)

    def c1(k):
        if k == 5:
            for c in range(CHUNKS):
                got(SLOT[5], c)

        hi, lo = pt[k, 0], pt[k, 1]

        def part(where):
            return (
                dot_nn(ownt[0, where], hi) + dot_nn(ownt[0, where], lo) + dot_nn(ownt[1, where], hi)
            )

        pbo[k] = part(other)
        core_copy(k).start()
        hb[k] = part(mine)

    def c2(k):
        core_copy(k).wait_recv()
        hb[k] += cb[k]
        for n in range(3):
            x_copy(k, n).start()

    def c3(k):
        for n in range(3):
            x_copy(k, n).wait_recv()
        qb[k] = (hb[k, quarter(at.x)] + xb[k, 0]) + (xb[k, 1] + xb[k, 2])
        z_copy(k).start()

    def c4(k):
        z_copy(k).wait_recv()
        summed = qb[k, pl.ds(pl.multiple_of(at.low * 32, 32), 32)] + zb[k]
        energy = eb[0, 0:1, 0:1] + eb[k, 0:1, 0:1]
        denom = energy - vcol[own_rows, 0:1] - vir_ref[...]
        amplitude = summed / denom
        hi = amplitude.astype(jnp.bfloat16)
        am[k, 0, own_rows] = hi
        am[k, 1, own_rows] = (amplitude - hi.astype(jnp.float32)).astype(jnp.bfloat16)
        az_copy(k).start()

    def c5(k):
        az_copy(k).wait_recv()
        for n in range(3):
            ax_copy(k, n).start()
        ac_copy(k, 0).start()

    def c6(k):
        for n in range(3):
            ax_copy(k, n).wait_recv()
            ac_copy(k, (3, 1, 2)[n]).start()

    def c7(k):
        for n in range(4):
            ac_copy(k, n).wait_recv()
        hi, lo = pt[k, 0], pt[k, 1]
        out_ref[...] += dot_nt(hi, am[k, 0]) + dot_nt(hi, am[k, 1]) + dot_nt(lo, am[k, 0])
        energy = eb[0, 0:1, 0:1] + eb[k, 0:1, 0:1]
        total = jnp.zeros((1, 1), jnp.float32)
        for r in range(4):
            band = pl.ds(r * 128, 128)
            a = am[k, 0, band].astype(jnp.float32) + am[k, 1, band].astype(jnp.float32)
            b = am[k, 0, :, band].astype(jnp.float32) + am[k, 1, :, band].astype(jnp.float32)
            denom = energy - vcol[band, 0:1] - vir_ref[...]
            total += jnp.sum(a * denom * (2.0 * a - b.T), axis=(0, 1), keepdims=True)
        lane = lax.broadcasted_iota(jnp.int32, en_ref.shape, 1)
        en_ref[...] += jnp.where(lane == ORDER[k], total / (512 * 512), 0.0)

    def fill():
        fb[at.occ] = fit_ref[...]
        ib[at.fit] = int_ref[...]
        eb[0] = jnp.broadcast_to(occ_ref[...], (8, 128))
        out_ref[...] = jnp.zeros_like(out_ref)
        en_ref[...] = jnp.zeros_like(en_ref)
        vcol[...] = jnp.broadcast_to(vir_ref[...], (128, 512)).T
        for d in range(1, 6):
            energy_copy(d).start()

    def relay(d, c, only):
        slot = SLOT.get(d, {"V": VIA, "N": NEXT}.get(d))

        @pl.when(y == only)
        def _():
            got(slot, c)
            for n in range(len(ROUTES)):
                if ROUTES[n][0] == slot and takes(n, only, c):
                    route(n, c).start()

    def own_z(c):
        f_copy(0, c).start()
        f_copy(1, c).start()

    stages = {1: c1, 2: c2, 3: c3, 4: c4, 5: c5, 6: c6, 7: c7}
    steps = {
        "oz": own_z,
        "oy": lambda c: f_spread(0, c),
        "a1": lambda c: f_near(1, c),
        "a3": lambda c: f_near(3, c),
        "a2": f_far,
        "b": f_side,
        "jl": lambda h: j_send((0, 0, h, "low")),
        "jo": j_own,
        "jg": j_low,
        "jr": j_relay,
        "jt": j_last,
        "f1": fit_most,
        "f2": fit_rest,
        "py": lambda c: send_on(0, c, False),
        "g": relay,
        "c": lambda j, k: stages[j](k),
    }
    filled = False
    for name, *rest in PLAN:
        if not filled and name not in ("oz", "oy", "jl", "jo"):
            fill()
            filled = True
        if (name, *rest) == ("f2", 3):
            for d in range(1, 6):
                energy_copy(d).wait_recv()
        steps[name](*rest)

    for n in range(20):
        lax.fori_loop(0, CHUNKS, lambda c, _: (f_copy(n, c).wait_send(), _)[1], 0)
    for n in range(len(HOPS)):
        j_copy(n).wait_send()
    for n in range(len(ROUTES)):
        for c in range(CHUNKS):
            pl.when(takes(n, y, c))(lambda n=n, c=c: route(n, c).wait_send())
    for d in range(1, 6):
        energy_copy(d).wait_send()

    def finish(k, carry):
        core_copy(k).wait_send()
        z_copy(k).wait_send()
        az_copy(k).wait_send()
        for n in range(3):
            x_copy(k, n).wait_send()
            ax_copy(k, n).wait_send()
        for n in range(4):
            ac_copy(k, n).wait_send()
        return carry

    lax.fori_loop(0, 6, finish, 0)


def run(fitting, integrals, occ_energy, vir_energy):
    f32, bf16 = jnp.float32, jnp.bfloat16
    dma = pltpu.SemaphoreType.DMA
    return pl.pallas_call(
        kernel,
        out_shape=(
            jax.ShapeDtypeStruct((512, 512), f32),
            jax.ShapeDtypeStruct((8, 128), f32),
        ),
        in_specs=[pl.BlockSpec(memory_space=pltpu.VMEM)] * 4,
        out_specs=[pl.BlockSpec(memory_space=pltpu.VMEM)] * 2,
        scratch_shapes=[
            pltpu.VMEM((16, 512, 512), bf16),
            pltpu.VMEM((16, 512, 512), bf16),
            pltpu.VMEM((128, 512), f32),
            pltpu.VMEM((6, 2, 512, 512), bf16),
            pltpu.VMEM((2, 2, 256, 512), bf16),
            pltpu.VMEM((2, 512, 512), bf16),
            pltpu.VMEM((6, 256, 512), f32),
            pltpu.VMEM((6, 256, 512), f32),
            pltpu.VMEM((6, 256, 512), f32),
            pltpu.VMEM((6, 3, 64, 512), f32),
            pltpu.VMEM((6, 64, 512), f32),
            pltpu.VMEM((6, 32, 512), f32),
            pltpu.VMEM((6, 2, 512, 512), bf16),
            pltpu.VMEM((6, 8, 128), f32),
            pltpu.VMEM((512, 128), f32),
            dma((20, CHUNKS)), dma((16, CHUNKS, 2)),
            dma((len(HOPS),)), dma((16, 2)),
            dma((len(ROUTES), CHUNKS)), dma((8, CHUNKS)),
            dma((6,)), dma((6,)),
            dma((6,)), dma((6,)),
            dma((6, 3)), dma((6, 3)),
            dma((6,)), dma((6,)),
            dma((6,)), dma((6,)),
            dma((6, 3)), dma((6, 3)),
            dma((6, 4)), dma((6, 4)),
        ],
        compiler_params=pltpu.CompilerParams(
            collective_id=0, has_side_effects=True, vmem_limit_bytes=60 * 1024 * 1024
        ),
    )(fitting, integrals, occ_energy, vir_energy)


def body(integrals, fitting, occ_energy, vir_energy):
    density, energies = run(fitting, integrals[:, 0, :], occ_energy[:, None], vir_energy[None, :])
    return (density[:, None, :], energies[0:1, 0:STOPS])


def solution(mesh):
    placed = (P("fit", "occ", None), P("fit", "occ"), P("occ"), P())
    return jax.shard_map(
        body,
        mesh=mesh,
        in_specs=placed,
        out_specs=(P("fit", "occ", None), P("occ", None)),
        check_vma=False,
    )
```

```python
import jax
import jax.numpy as jnp
from jax import lax
from jax.experimental import pallas as pl
from jax.experimental.pallas import tpu as pltpu
from jax.sharding import PartitionSpec as P

STOPS = 6
MESH = pl.DeviceIdType.MESH


class Place:
    def __init__(self):
        self.occ = lax.axis_index("occ")
        self.fit = lax.axis_index("fit")
        self.z, self.y = self.occ // 4, self.occ % 4
        self.x, self.low, self.core = self.fit // 4, (self.fit // 2) % 2, self.fit % 2

    def o(self, dz, dy):
        return ((self.z + dz + 4) % 4) * 4 + (self.y + dy + 4) % 4

    def f(self, dx, flip_low=0, flip_core=0):
        low = self.low if not flip_low else 1 - self.low
        core = self.core if not flip_core else 1 - self.core
        return ((self.x + dx + 4) % 4) * 4 + low * 2 + core


def entry_barrier(peers):
    barrier = pltpu.get_barrier_semaphore()
    for occ, fit in peers:
        pl.semaphore_signal(barrier, inc=1, device_id={"occ": occ, "fit": fit}, device_id_type=MESH)
    pl.semaphore_wait(barrier, len(peers))


ORDER = (0, 4, 1, 3, 2, 5)
SLOT = {d: k for k, d in enumerate(ORDER)}
VIA, NEXT = 6, 7
CHUNKS = 4
ROUTES = (
    (0, SLOT[4], -1, 0),
    (0, SLOT[1], 0, -1),
    (0, SLOT[3], 0, 1),
    (0, VIA, 0, -1),
    (0, VIA, 1, 0),
    (SLOT[1], SLOT[2], 0, -1),
    (SLOT[4], SLOT[1], 0, -1),
    (SLOT[4], SLOT[3], 0, 1),
    (SLOT[4], SLOT[5], 0, -1),
    (SLOT[3], SLOT[2], 0, 1),
    (SLOT[2], SLOT[5], 0, 1),
    (VIA, NEXT, 1, 0),
    (NEXT, SLOT[5], 1, 0),
    (NEXT, SLOT[5], 0, -1),
)
HOPS = tuple((0, 0, h, to) for h in (0, 1) for to in ("low", 1, -1)) + tuple(
    (0, 1, h, to) for h in (0, 1) for to in (1, -1)
) + ((0, 0, None, "core"), (0, 1, None, "core")) + tuple(
    hop
    for low in (0, 1)
    for hop in (
        (1, low, 0, -1),
        (-1, low, 1, 1),
        (1, low, None, "core"),
        (-1, low, None, "core"),
        (2, low, None, "core"),
    )
)
LOW_FIRST = (2, 4)
PLAN = (
    ("oy", 0), ("oz", 0), ("oy", 2), ("jo",), ("oy", 3), ("oy", 1), ("jl", 0), ("jl", 1), ("oz", 1),
    ("oz", 2), ("a3", 0), ("jr", 0, 0), ("b", 0, 3), ("jr", 1, 0), ("oz", 3), ("b", 0, 1),
    ("jg", 0), ("b", 3, 0), ("a1", 1), ("b", 0, 0), ("a1", 0), ("jg", 1), ("a3", 1), ("a1", 3),
    ("jr", 0, 1), ("jt", 0), ("a3", 2), ("jr", 1, 1), ("a2", 0), ("b", 1, 1), ("b", 1, 0),
    ("jt", 1), ("b", 2, 0), ("b", 3, 1), ("a1", 2), ("f1", 0), ("a2", 1), ("f2", 0), ("a2", 2),
    ("b", 2, 1), ("b", 0, 2), ("a3", 3), ("b", 3, 2), ("b", 1, 2), ("f1", 1), ("b", 2, 2),
    ("f2", 1), ("a2", 3), ("b", 1, 3), ("f1", 2), ("b", 3, 3), ("f2", 2), ("b", 2, 3), ("py", 0),
    ("g", 4, 0, 1), ("py", 1), ("py", 2), ("g", 4, 0, 0), ("g", 4, 0, 2), ("g", "V", 0, 3),
    ("f1", 3), ("g", 4, 1, 1), ("f2", 3), ("c", 1, 0), ("py", 3), ("g", "V", 1, 3), ("g", 4, 1, 0),
    ("g", 3, 0, 0), ("c", 2, 0), ("g", 4, 2, 3), ("g", 4, 2, 0), ("g", 1, 0, 1), ("g", "N", 0, 3),
    ("g", 3, 0, 1), ("g", 3, 1, 0), ("g", 1, 1, 0), ("g", 2, 0, 3), ("g", 3, 1, 1), ("g", 1, 1, 1),
    ("g", 4, 2, 1), ("g", 4, 1, 2), ("c", 3, 0), ("g", 3, 0, 2), ("g", 2, 0, 2), ("g", 3, 0, 3),
    ("c", 4, 0), ("g", "V", 2, 0), ("g", 4, 1, 3), ("g", 4, 2, 2), ("g", 4, 3, 3), ("g", 4, 3, 0),
    ("g", 4, 3, 2), ("g", 4, 0, 3), ("g", 4, 3, 1), ("c", 1, 1), ("g", 1, 0, 3), ("g", 2, 1, 2),
    ("g", 2, 0, 0), ("g", 3, 2, 1), ("c", 2, 1), ("g", "V", 3, 0), ("g", 1, 2, 1), ("g", 1, 2, 0),
    ("g", 1, 1, 2), ("g", 1, 0, 0), ("g", 3, 1, 2), ("g", 3, 2, 3), ("g", 3, 3, 0), ("c", 5, 0),
    ("g", 3, 1, 3), ("g", 2, 1, 1), ("g", 1, 2, 3), ("g", 3, 3, 3), ("g", 1, 3, 1),
    ("g", "N", 1, 3), ("g", 1, 2, 2), ("g", 1, 0, 2), ("g", 1, 3, 0), ("g", 3, 2, 2),
    ("g", 1, 3, 3), ("g", 1, 3, 2), ("g", 3, 2, 0), ("g", 1, 1, 3), ("c", 1, 2), ("g", 3, 3, 1),
    ("g", 3, 3, 2), ("c", 1, 3), ("c", 3, 1), ("c", 2, 2), ("g", 2, 1, 3), ("c", 2, 3),
    ("g", 2, 3, 1), ("g", 2, 2, 2), ("c", 4, 1), ("g", "N", 2, 0), ("g", 2, 2, 1), ("g", 2, 2, 0),
    ("g", 2, 0, 1), ("g", "N", 3, 0), ("g", 2, 3, 0), ("g", 2, 2, 3), ("c", 3, 2), ("g", 2, 3, 2),
    ("g", 2, 3, 3), ("g", 2, 1, 0), ("c", 1, 4), ("c", 5, 1), ("c", 3, 3), ("c", 2, 4), ("c", 4, 2),
    ("c", 4, 3), ("c", 1, 5), ("c", 3, 4), ("c", 2, 5), ("c", 6, 1), ("c", 6, 0), ("c", 5, 2),
    ("c", 4, 4), ("c", 5, 3), ("c", 7, 1), ("c", 6, 2), ("c", 3, 5), ("c", 4, 5), ("c", 5, 4),
    ("c", 5, 5), ("c", 7, 2), ("c", 6, 3), ("c", 7, 0), ("c", 6, 4), ("c", 7, 3), ("c", 6, 5),
    ("c", 7, 4), ("c", 7, 5),
)


def carries(y, c):
    return ((y == 3) & (c < 2)) | ((y == 0) & (c >= 2))


def takes(route, y, c):
    return (
        True,
        y > 0,
        y == 3,
        (y == 0) & (c < 2),
        (y == 0) & (c >= 2),
        y == 1,
        y == 0,
        y < 3,
        y >= 2,
        y < 3,
        y == 3,
        carries(y, c),
        (y == 3) & (c < 2),
        (y == 0) & (c >= 2),
    )[route]


def dot_nt(a, b):
    return lax.dot_general(a, b, (((1,), (1,)), ((), ())), preferred_element_type=jnp.float32)


def dot_nn(a, b):
    return jnp.dot(a, b, preferred_element_type=jnp.float32)


def kernel(
    fit_ref, int_ref, occ_ref, vir_ref, out_ref, en_ref,
    fb, ib, acc, pt, spare, ownt, pbo, hb, cb, xb, qb, zb, qz, zz, am, eb, vcol,
    fs, fr, js, jr, rs, rr, es, er, cs, cr, xs, xr, zs, zr, azs, azr, axs, axr, acs, acr,
):
    at = Place()
    y = at.y
    core_peer, low_peer = at.f(0, 0, 1), at.f(0, 1)
    x_peers = (at.f(1), at.f(-1), at.f(2))
    ahead = [(at.occ + d) % 16 for d in range(1, 6)]
    behind = [(at.occ + 16 - d) % 16 for d in range(1, 6)]
    entry_barrier(
        [(o, at.fit) for o in ahead + behind]
        + [(at.occ, f) for f in x_peers + (core_peer, low_peer)]
    )

    def remote(src, dst, ssem, rsem, occ, fit):
        return pltpu.make_async_remote_copy(
            src_ref=src, dst_ref=dst, send_sem=ssem, recv_sem=rsem,
            device_id={"occ": occ, "fit": fit}, device_id_type=MESH,
        )

    def rows(c):
        return pl.ds(pl.multiple_of(c * 128, 128), 128)

    def rows_of(c, half):
        if half is None:
            return rows(c)
        return pl.ds(pl.multiple_of(c * 128 + half * 64, 64), 64)

    def f_copy(n, c):
        if n < 2:
            slot, half, own, to = at.occ, None, True, at.o((1, -1)[n], 0)
        elif n < 4:
            slot, half, own, to = at.o((1, -1)[n - 2], 0), n - 2, False, at.o((-1, 1)[n - 2], 0)
        elif n < 12:
            dz, up = (n - 4) // 2, (n - 4) % 2
            slot, half, own, to = at.o(dz, 0), None, dz == 0, at.o(0, (1, -1)[up])
        else:
            dz, up = (n - 12) // 2, (n - 12) % 2
            slot, half, own, to = at.o(dz, (1, -1)[up]), up, False, at.o(0, (-1, 1)[up])
        where = rows_of(c, half)
        src = fit_ref.at[where] if own else fb.at[slot, where]
        return remote(src, fb.at[slot, where], fs.at[n, c], fr.at[slot, c, half or 0], to, at.fit)

    def f_got(dz, dy, c):
        slot = at.o(dz, dy)
        for half in ((0, 1) if dy == 2 or (dz == 2 and dy == 0) else (None,)):
            part = fb.at[slot, rows_of(c, half)]
            remote(part, part, fs.at[0, 0], fr.at[slot, c, half or 0], at.occ, at.fit).wait_recv()

    def f_spread(dz, c):
        f_copy(4 + 2 * dz, c).start()
        f_copy(5 + 2 * dz, c).start()

    def f_near(dz, c):
        f_got(dz, 0, c)
        f_copy(2 if dz == 1 else 3, c).start()
        f_spread(dz, c)

    def f_far(c):
        f_got(2, 0, c)
        f_spread(2, c)

    def f_side(dz, c):
        f_got(dz, 1, c)
        f_got(dz, 3, c)
        f_copy(12 + 2 * dz, c).start()
        f_copy(13 + 2 * dz, c).start()

    def j_copy(n):
        dx, flip_low, half, to = HOPS[n]
        slot = at.f(dx, flip_low)
        where = pl.ds(0, 512) if half is None else pl.ds(half * 256, 256)
        src = int_ref.at[where] if (dx, flip_low) == (0, 0) else ib.at[slot, where]
        fit = {"low": low_peer, "core": core_peer, 1: at.f(1), -1: at.f(-1)}[to]
        return remote(src, ib.at[slot, where], js.at[n], jr.at[slot, half or 0], at.occ, fit)

    def j_send(*hops):
        for hop in hops:
            j_copy(HOPS.index(hop)).start()

    def j_got(slot, half):
        where = pl.ds(0, 512) if half is None else pl.ds(half * 256, 256)
        part = ib.at[slot, where]
        remote(part, part, js.at[0], jr.at[slot, half or 0], at.occ, at.fit).wait_recv()

    def j_own():
        for h in (0, 1):
            j_send((0, 0, h, -1), (0, 0, 1 - h, 1))
        j_send((0, 0, None, "core"))

    def j_low(h):
        j_got(at.f(0, 1), h)
        j_send((0, 1, h, -1), (0, 1, h, 1))
        if h == 1:
            j_send((0, 1, None, "core"))

    def j_relay(second, low):
        j_got(at.f(1, low), second)
        j_got(at.f(-1, low), 1 - second)
        if second:
            j_send((1, low, None, "core"), (-1, low, None, "core"))
        else:
            j_send((1, low, 0, -1), (-1, low, 1, 1))

    def j_last(low):
        j_got(at.f(2, low), 0)
        j_got(at.f(2, low), 1)
        j_send((2, low, None, "core"))

    def j_core():
        for low in (0, 1):
            for dx in (0, 1, -1, 2):
                j_got(at.f(dx, low, 1), None)

    def place(slot, c):
        if slot >= VIA:
            return spare.at[slot - VIA, :, pl.ds(pl.multiple_of((c % 2) * 128, 128), 128)]
        return pt.at[slot, :, rows(c)]

    def route(n, c):
        src, dst, dz, dy = ROUTES[n]
        return remote(place(src, c), place(dst, c), rs.at[n, c], rr.at[dst, c], at.o(dz, dy), at.fit)

    def send_on(slot, c, over_z=None):
        for n, (source, _, dz, _) in enumerate(ROUTES):
            if source == slot and over_z in (None, dz != 0):
                pl.when(takes(n, y, c))(lambda n=n: route(n, c).start())

    def got(slot, c):
        part = place(slot, c)
        remote(part, part, rs.at[0, 0], rr.at[slot, c], at.occ, at.fit).wait_recv()

    def energy_copy(d):
        k = SLOT[d]
        return remote(eb.at[0], eb.at[k], es.at[k], er.at[k], behind[d - 1], at.fit)

    def add(dy, c):
        def one(dz, carry):
            slot = at.o(dz, dy)
            acc[...] += dot_nn(fb[slot, rows(c)], ib[slot])
            return carry

        lax.fori_loop(0, 4, one, 0)

    def fit_most(c):
        if c == 0:
            j_core()
        acc[...] = jnp.zeros_like(acc)
        for dy in (0, 1, 3):
            add(dy, c)

    def fit_rest(c):
        for dz in range(4):
            f_got(dz, 2, c)
        add(2, c)
        whole = acc[...]
        hi = whole.astype(jnp.bfloat16)
        low = whole - hi.astype(jnp.float32)
        pt[0, 0, rows(c)] = hi
        pt[0, 1, rows(c)] = low.astype(jnp.bfloat16)
        ownt[0, :, rows(c)] = hi.astype(jnp.float32).T.astype(jnp.bfloat16)
        ownt[1, :, rows(c)] = low.T.astype(jnp.bfloat16)
        send_on(0, c, True)

    mine = pl.ds(pl.multiple_of(at.core * 256, 256), 256)
    other = pl.ds(pl.multiple_of((1 - at.core) * 256, 256), 256)

    def quarter(x):
        return pl.ds(pl.multiple_of(x * 64, 64), 64)

    def core_copy(k):
        return remote(pbo.at[k], cb.at[k], cs.at[k], cr.at[k], at.occ, core_peer)

    def x_copy(k, n):
        to = (at.x + (1, 3, 2)[n]) % 4
        if k in LOW_FIRST:
            src, dst = qz.at[k, pl.ds(pl.multiple_of(to * 32, 32), 32)], xb.at[k, n, pl.ds(0, 32)]
        else:
            src, dst = hb.at[k, quarter(to)], xb.at[k, n]
        return remote(src, dst, xs.at[k, n], xr.at[k, n], at.occ, x_peers[n])

    def half_of(low):
        return pl.ds(pl.multiple_of(low * 128, 128), 128)

    def z_copy(k):
        if k in LOW_FIRST:
            src, dst = hb.at[k, half_of(1 - at.low)], zz.at[k]
        else:
            half = pl.ds(pl.multiple_of((1 - at.low) * 32, 32), 32)
            src, dst = qb.at[k, half], zb.at[k]
        return remote(src, dst, zs.at[k], zr.at[k], at.occ, low_peer)

    def block(x, core):
        return pl.ds(pl.multiple_of(core * 256 + x * 64, 64), 64)

    def own_rows(k):
        if k in LOW_FIRST:
            start = at.core * 256 + at.low * 128 + at.x * 32
        else:
            start = at.core * 256 + at.x * 64 + at.low * 32
        return pl.ds(pl.multiple_of(start, 32), 32)

    def low_rows(low):
        return pl.ds(pl.multiple_of(at.core * 256 + low * 128, 128), 128)

    def az_copy(k):
        part = am.at[k, :, low_rows(at.low) if k in LOW_FIRST else own_rows(k)]
        return remote(part, part, azs.at[k], azr.at[k], at.occ, low_peer)

    def ax_copy(k, n):
        part = am.at[k, :, own_rows(k) if k in LOW_FIRST else block(at.x, at.core)]
        return remote(part, part, axs.at[k, n], axr.at[k, n], at.occ, x_peers[n])

    def ac_parts(k):
        return 2 if k in LOW_FIRST else 4

    def ac_copy(k, n):
        if k in LOW_FIRST:
            part = am.at[k, :, low_rows(at.low if n == 0 else 1 - at.low)]
        else:
            part = am.at[k, :, block((at.x + n) % 4, at.core)]
        return remote(part, part, acs.at[k, n], acr.at[k, n], at.occ, core_peer)

    def c1(k):
        if k == 5:
            for c in range(CHUNKS):
                got(SLOT[5], c)

        hi, lo = pt[k, 0], pt[k, 1]

        def part(where):
            return (
                dot_nn(ownt[0, where], hi) + dot_nn(ownt[0, where], lo) + dot_nn(ownt[1, where], hi)
            )

        pbo[k] = part(other)
        core_copy(k).start()
        hb[k] = part(mine)

    def start_x(copy, k):
        for n in range(3):
            copy(k, n).start()

    def wait_x(copy, k):
        for n in range(3):
            copy(k, n).wait_recv()

    def c2(k):
        core_copy(k).wait_recv()
        hb[k] += cb[k]
        if k in LOW_FIRST:
            z_copy(k).start()
        else:
            start_x(x_copy, k)

    def c3(k):
        if k in LOW_FIRST:
            z_copy(k).wait_recv()
            qz[k] = hb[k, half_of(at.low)] + zz[k]
            start_x(x_copy, k)
        else:
            wait_x(x_copy, k)
            qb[k] = (hb[k, quarter(at.x)] + xb[k, 0]) + (xb[k, 1] + xb[k, 2])
            z_copy(k).start()

    def c4(k):
        if k in LOW_FIRST:
            wait_x(x_copy, k)
            own = qz[k, pl.ds(pl.multiple_of(at.x * 32, 32), 32)]
            summed = (own + xb[k, 0, 0:32]) + (xb[k, 1, 0:32] + xb[k, 2, 0:32])
        else:
            z_copy(k).wait_recv()
            summed = qb[k, pl.ds(pl.multiple_of(at.low * 32, 32), 32)] + zb[k]
        energy = eb[0, 0:1, 0:1] + eb[k, 0:1, 0:1]
        denom = energy - vcol[own_rows(k), 0:1] - vir_ref[...]
        amplitude = summed / denom
        hi = amplitude.astype(jnp.bfloat16)
        am[k, 0, own_rows(k)] = hi
        am[k, 1, own_rows(k)] = (amplitude - hi.astype(jnp.float32)).astype(jnp.bfloat16)
        if k in LOW_FIRST:
            start_x(ax_copy, k)
        else:
            az_copy(k).start()

    def c5(k):
        if k in LOW_FIRST:
            wait_x(ax_copy, k)
            az_copy(k).start()
        else:
            az_copy(k).wait_recv()
            start_x(ax_copy, k)
        ac_copy(k, 0).start()

    def c6(k):
        if k in LOW_FIRST:
            az_copy(k).wait_recv()
            ac_copy(k, 1).start()
        else:
            for n in range(3):
                ax_copy(k, n).wait_recv()
                ac_copy(k, (3, 1, 2)[n]).start()

    def c7(k):
        for n in range(ac_parts(k)):
            ac_copy(k, n).wait_recv()
        hi, lo = pt[k, 0], pt[k, 1]
        out_ref[...] += dot_nt(hi, am[k, 0]) + dot_nt(hi, am[k, 1]) + dot_nt(lo, am[k, 0])
        energy = eb[0, 0:1, 0:1] + eb[k, 0:1, 0:1]
        total = jnp.zeros((1, 1), jnp.float32)
        for r in range(4):
            band = pl.ds(r * 128, 128)
            a = am[k, 0, band].astype(jnp.float32) + am[k, 1, band].astype(jnp.float32)
            b = am[k, 0, :, band].astype(jnp.float32) + am[k, 1, :, band].astype(jnp.float32)
            denom = energy - vcol[band, 0:1] - vir_ref[...]
            total += jnp.sum(a * denom * (2.0 * a - b.T), axis=(0, 1), keepdims=True)
        lane = lax.broadcasted_iota(jnp.int32, en_ref.shape, 1)
        en_ref[...] += jnp.where(lane == ORDER[k], total / (512 * 512), 0.0)

    def fill():
        fb[at.occ] = fit_ref[...]
        ib[at.fit] = int_ref[...]
        eb[0] = jnp.broadcast_to(occ_ref[...], (8, 128))
        out_ref[...] = jnp.zeros_like(out_ref)
        en_ref[...] = jnp.zeros_like(en_ref)
        vcol[...] = jnp.broadcast_to(vir_ref[...], (128, 512)).T
        for d in range(1, 6):
            energy_copy(d).start()

    def relay(d, c, only):
        slot = SLOT.get(d, {"V": VIA, "N": NEXT}.get(d))

        @pl.when(y == only)
        def _():
            got(slot, c)
            for n in range(len(ROUTES)):
                if ROUTES[n][0] == slot and takes(n, only, c):
                    route(n, c).start()

    def own_z(c):
        f_copy(0, c).start()
        f_copy(1, c).start()

    stages = {1: c1, 2: c2, 3: c3, 4: c4, 5: c5, 6: c6, 7: c7}
    steps = {
        "oz": own_z,
        "oy": lambda c: f_spread(0, c),
        "a1": lambda c: f_near(1, c),
        "a3": lambda c: f_near(3, c),
        "a2": f_far,
        "b": f_side,
        "jl": lambda h: j_send((0, 0, h, "low")),
        "jo": j_own,
        "jg": j_low,
        "jr": j_relay,
        "jt": j_last,
        "f1": fit_most,
        "f2": fit_rest,
        "py": lambda c: send_on(0, c, False),
        "g": relay,
        "c": lambda j, k: stages[j](k),
    }
    filled = False
    for name, *rest in PLAN:
        if not filled and name not in ("oz", "oy", "jl", "jo"):
            fill()
            filled = True
        if (name, *rest) == ("f2", 3):
            for d in range(1, 6):
                energy_copy(d).wait_recv()
        steps[name](*rest)

    for n in range(20):
        lax.fori_loop(0, CHUNKS, lambda c, _: (f_copy(n, c).wait_send(), _)[1], 0)
    for n in range(len(HOPS)):
        j_copy(n).wait_send()
    for n in range(len(ROUTES)):
        for c in range(CHUNKS):
            pl.when(takes(n, y, c))(lambda n=n, c=c: route(n, c).wait_send())
    for d in range(1, 6):
        energy_copy(d).wait_send()

    for k in range(6):
        core_copy(k).wait_send()
        z_copy(k).wait_send()
        az_copy(k).wait_send()
        for n in range(3):
            x_copy(k, n).wait_send()
            ax_copy(k, n).wait_send()
        for n in range(ac_parts(k)):
            ac_copy(k, n).wait_send()


def run(fitting, integrals, occ_energy, vir_energy):
    f32, bf16 = jnp.float32, jnp.bfloat16
    dma = pltpu.SemaphoreType.DMA
    return pl.pallas_call(
        kernel,
        out_shape=(
            jax.ShapeDtypeStruct((512, 512), f32),
            jax.ShapeDtypeStruct((8, 128), f32),
        ),
        in_specs=[pl.BlockSpec(memory_space=pltpu.VMEM)] * 4,
        out_specs=[pl.BlockSpec(memory_space=pltpu.VMEM)] * 2,
        scratch_shapes=[
            pltpu.VMEM((16, 512, 512), bf16),
            pltpu.VMEM((16, 512, 512), bf16),
            pltpu.VMEM((128, 512), f32),
            pltpu.VMEM((6, 2, 512, 512), bf16),
            pltpu.VMEM((2, 2, 256, 512), bf16),
            pltpu.VMEM((2, 512, 512), bf16),
            pltpu.VMEM((6, 256, 512), f32),
            pltpu.VMEM((6, 256, 512), f32),
            pltpu.VMEM((6, 256, 512), f32),
            pltpu.VMEM((6, 3, 64, 512), f32),
            pltpu.VMEM((6, 64, 512), f32),
            pltpu.VMEM((6, 32, 512), f32),
            pltpu.VMEM((6, 128, 512), f32),
            pltpu.VMEM((6, 128, 512), f32),
            pltpu.VMEM((6, 2, 512, 512), bf16),
            pltpu.VMEM((6, 8, 128), f32),
            pltpu.VMEM((512, 128), f32),
            dma((20, CHUNKS)), dma((16, CHUNKS, 2)),
            dma((len(HOPS),)), dma((16, 2)),
            dma((len(ROUTES), CHUNKS)), dma((8, CHUNKS)),
            dma((6,)), dma((6,)),
            dma((6,)), dma((6,)),
            dma((6, 3)), dma((6, 3)),
            dma((6,)), dma((6,)),
            dma((6,)), dma((6,)),
            dma((6, 3)), dma((6, 3)),
            dma((6, 4)), dma((6, 4)),
        ],
        compiler_params=pltpu.CompilerParams(
            collective_id=0, has_side_effects=True, vmem_limit_bytes=60 * 1024 * 1024
        ),
    )(fitting, integrals, occ_energy, vir_energy)


def body(integrals, fitting, occ_energy, vir_energy):
    density, energies = run(fitting, integrals[:, 0, :], occ_energy[:, None], vir_energy[None, :])
    return (density[:, None, :], energies[0:1, 0:STOPS])


def solution(mesh):
    placed = (P("fit", "occ", None), P("fit", "occ"), P("occ"), P())
    return jax.shard_map(
        body,
        mesh=mesh,
        in_specs=placed,
        out_specs=(P("fit", "occ", None), P("occ", None)),
        check_vma=False,
    )
```

```python
import jax
import jax.numpy as jnp
from jax import lax
from jax.experimental import pallas as pl
from jax.experimental.pallas import tpu as pltpu
from jax.sharding import PartitionSpec as P

STOPS = 6
MESH = pl.DeviceIdType.MESH


class Place:
    def __init__(self):
        self.occ = lax.axis_index("occ")
        self.fit = lax.axis_index("fit")
        self.z, self.y = self.occ // 4, self.occ % 4
        self.x, self.low, self.core = self.fit // 4, (self.fit // 2) % 2, self.fit % 2

    def o(self, dz, dy):
        return ((self.z + dz + 4) % 4) * 4 + (self.y + dy + 4) % 4

    def f(self, dx, flip_low=0, flip_core=0):
        low = self.low if not flip_low else 1 - self.low
        core = self.core if not flip_core else 1 - self.core
        return ((self.x + dx + 4) % 4) * 4 + low * 2 + core


def entry_barrier(peers):
    barrier = pltpu.get_barrier_semaphore()
    for occ, fit in peers:
        pl.semaphore_signal(barrier, inc=1, device_id={"occ": occ, "fit": fit}, device_id_type=MESH)
    pl.semaphore_wait(barrier, len(peers))


ORDER = (0, 4, 1, 3, 2, 5)
SLOT = {d: k for k, d in enumerate(ORDER)}
VIA, NEXT = 6, 7
CHUNKS = 4
ROUTES = (
    (0, SLOT[4], -1, 0),
    (0, SLOT[1], 0, -1),
    (0, SLOT[3], 0, 1),
    (0, VIA, 0, -1),
    (0, VIA, 1, 0),
    (SLOT[1], SLOT[2], 0, -1),
    (SLOT[4], SLOT[1], 0, -1),
    (SLOT[4], SLOT[3], 0, 1),
    (SLOT[4], SLOT[5], 0, -1),
    (SLOT[3], SLOT[2], 0, 1),
    (SLOT[2], SLOT[5], 0, 1),
    (VIA, NEXT, 1, 0),
    (NEXT, SLOT[5], 1, 0),
    (NEXT, SLOT[5], 0, -1),
)
HOPS = tuple((0, 0, h, to) for h in (0, 1) for to in ("low", 1, -1)) + tuple(
    (0, 1, h, to) for h in (0, 1) for to in (1, -1)
) + ((0, 0, None, "core"), (0, 1, None, "core")) + tuple(
    hop
    for low in (0, 1)
    for hop in (
        (1, low, 0, -1),
        (-1, low, 1, 1),
        (1, low, None, "core"),
        (-1, low, None, "core"),
        (2, low, None, "core"),
    )
)
LOW_FIRST = (2, 4)
PLAN = (
    ("oy", 2), ("oy", 1), ("oz", 0), ("oy", 0), ("jo",), ("jl", 0), ("jl", 1), ("oz", 1), ("oy", 3),
    ("jr", 0, 0), ("oz", 2), ("a3", 0), ("a1", 0), ("jg", 0), ("oz", 3), ("a1", 1), ("b", 0, 0),
    ("b", 0, 1), ("b", 0, 3), ("b", 3, 0), ("jt", 0), ("jg", 1), ("b", 1, 1), ("a3", 1), ("a1", 3),
    ("jr", 0, 1), ("a3", 2), ("jr", 1, 1), ("jr", 1, 0), ("a2", 0), ("b", 3, 1), ("b", 1, 0),
    ("jt", 1), ("b", 2, 0), ("b", 0, 2), ("a1", 2), ("f1", 0), ("a2", 1), ("f2", 0), ("a2", 2),
    ("b", 2, 1), ("a3", 3), ("b", 3, 2), ("b", 1, 2), ("f1", 1), ("f2", 1), ("a2", 3), ("b", 2, 2),
    ("b", 1, 3), ("py", 0), ("b", 3, 3), ("f1", 2), ("g", 4, 0, 1), ("b", 2, 3), ("py", 1),
    ("g", 4, 0, 0), ("f2", 2), ("g", 4, 0, 2), ("g", "V", 0, 3), ("f1", 3), ("g", 4, 1, 1),
    ("g", 3, 0, 2), ("g", 4, 1, 0), ("f2", 3), ("py", 2), ("g", "V", 1, 3), ("g", 3, 0, 0),
    ("g", 1, 0, 2), ("g", 3, 0, 1), ("c", 1, 0), ("g", 4, 1, 3), ("py", 3), ("g", 3, 1, 0),
    ("g", 4, 1, 2), ("g", 1, 0, 0), ("g", 3, 1, 1), ("c", 2, 0), ("g", 2, 0, 3), ("g", "V", 2, 0),
    ("g", 4, 2, 2), ("g", 4, 2, 1), ("g", 4, 0, 3), ("g", 4, 2, 3), ("g", 3, 1, 2), ("g", 1, 2, 0),
    ("g", "N", 0, 3), ("g", 1, 0, 1), ("g", 4, 2, 0), ("g", 1, 1, 1), ("g", 2, 1, 2),
    ("g", 3, 0, 3), ("g", 1, 2, 1), ("c", 3, 0), ("g", 4, 3, 3), ("g", 4, 3, 0), ("g", 4, 3, 1),
    ("g", 1, 2, 2), ("g", 4, 3, 2), ("c", 1, 1), ("c", 2, 1), ("g", 1, 3, 0), ("g", 1, 3, 1),
    ("g", 3, 2, 1), ("g", 1, 1, 2), ("g", 1, 1, 3), ("g", 1, 3, 2), ("g", 1, 2, 3), ("g", 3, 3, 0),
    ("g", 3, 2, 0), ("g", 3, 2, 2), ("g", 1, 0, 3), ("c", 4, 0), ("g", 3, 1, 3), ("g", 1, 3, 3),
    ("g", 1, 1, 0), ("c", 1, 2), ("g", "N", 1, 3), ("g", 3, 3, 3), ("g", 3, 3, 2), ("g", 3, 2, 3),
    ("g", 2, 0, 0), ("g", 2, 1, 3), ("g", 2, 0, 2), ("c", 5, 0), ("g", 3, 3, 1), ("g", 2, 1, 1),
    ("c", 2, 2), ("g", "V", 3, 0), ("c", 1, 3), ("c", 2, 3), ("c", 3, 1), ("g", 2, 0, 1),
    ("g", 2, 2, 3), ("c", 3, 2), ("g", 2, 2, 2), ("g", 2, 2, 0), ("c", 6, 0), ("c", 4, 1),
    ("g", 2, 2, 1), ("g", 2, 3, 2), ("g", "N", 2, 0), ("g", 2, 3, 0), ("g", 2, 3, 3),
    ("g", 2, 1, 0), ("g", 2, 3, 1), ("c", 1, 4), ("g", "N", 3, 0), ("c", 2, 4), ("c", 5, 1),
    ("c", 4, 2), ("c", 3, 3), ("c", 1, 5), ("c", 3, 4), ("c", 4, 3), ("c", 2, 5), ("c", 5, 2),
    ("c", 6, 1), ("c", 4, 4), ("c", 7, 1), ("c", 6, 2), ("c", 3, 5), ("c", 5, 3), ("c", 4, 5),
    ("c", 5, 4), ("c", 5, 5), ("c", 7, 2), ("c", 6, 3), ("c", 7, 0), ("c", 6, 4), ("c", 7, 3),
    ("c", 6, 5), ("c", 7, 4), ("c", 7, 5),
)


def carries(y, c):
    return ((y == 3) & (c < 2)) | ((y == 0) & (c >= 2))


def takes(route, y, c):
    return (
        True,
        y > 0,
        y == 3,
        (y == 0) & (c < 2),
        (y == 0) & (c >= 2),
        y == 1,
        y == 0,
        y < 3,
        y >= 2,
        y < 3,
        y == 3,
        carries(y, c),
        (y == 3) & (c < 2),
        (y == 0) & (c >= 2),
    )[route]


def dot_nt(a, b):
    return lax.dot_general(a, b, (((1,), (1,)), ((), ())), preferred_element_type=jnp.float32)


def dot_nn(a, b):
    return jnp.dot(a, b, preferred_element_type=jnp.float32)


def kernel(
    fit_ref, int_ref, occ_ref, vir_ref, out_ref, en_ref,
    fb, ib, acc, pt, spare, ownt, pbo, hb, cb, xb, qb, zb, qz, zz, am, eb, vcol,
    fs, fr, js, jr, rs, rr, es, er, cs, cr, xs, xr, zs, zr, azs, azr, axs, axr, acs, acr,
):
    at = Place()
    y = at.y
    core_peer, low_peer = at.f(0, 0, 1), at.f(0, 1)
    x_peers = (at.f(1), at.f(-1), at.f(2))
    ahead = [(at.occ + d) % 16 for d in range(1, 6)]
    behind = [(at.occ + 16 - d) % 16 for d in range(1, 6)]
    entry_barrier(
        [(o, at.fit) for o in ahead + behind]
        + [(at.occ, f) for f in x_peers + (core_peer, low_peer)]
    )

    def remote(src, dst, ssem, rsem, occ, fit):
        return pltpu.make_async_remote_copy(
            src_ref=src, dst_ref=dst, send_sem=ssem, recv_sem=rsem,
            device_id={"occ": occ, "fit": fit}, device_id_type=MESH,
        )

    def rows(c):
        return pl.ds(pl.multiple_of(c * 128, 128), 128)

    def rows_of(c, half):
        if half is None:
            return rows(c)
        return pl.ds(pl.multiple_of(c * 128 + half * 64, 64), 64)

    def f_copy(n, c):
        if n < 2:
            slot, half, own, to = at.occ, None, True, at.o((1, -1)[n], 0)
        elif n < 4:
            slot, half, own, to = at.o((1, -1)[n - 2], 0), n - 2, False, at.o((-1, 1)[n - 2], 0)
        elif n < 12:
            dz, up = (n - 4) // 2, (n - 4) % 2
            slot, half, own, to = at.o(dz, 0), None, dz == 0, at.o(0, (1, -1)[up])
        else:
            dz, up = (n - 12) // 2, (n - 12) % 2
            slot, half, own, to = at.o(dz, (1, -1)[up]), up, False, at.o(0, (-1, 1)[up])
        where = rows_of(c, half)
        src = fit_ref.at[where] if own else fb.at[slot, where]
        return remote(src, fb.at[slot, where], fs.at[n, c], fr.at[slot, c, half or 0], to, at.fit)

    def f_got(dz, dy, c):
        slot = at.o(dz, dy)
        for half in ((0, 1) if dy == 2 or (dz == 2 and dy == 0) else (None,)):
            part = fb.at[slot, rows_of(c, half)]
            remote(part, part, fs.at[0, 0], fr.at[slot, c, half or 0], at.occ, at.fit).wait_recv()

    def f_spread(dz, c):
        f_copy(4 + 2 * dz, c).start()
        f_copy(5 + 2 * dz, c).start()

    def f_near(dz, c):
        f_got(dz, 0, c)
        f_copy(2 if dz == 1 else 3, c).start()
        f_spread(dz, c)

    def f_far(c):
        f_got(2, 0, c)
        f_spread(2, c)

    def f_side(dz, c):
        f_got(dz, 1, c)
        f_got(dz, 3, c)
        f_copy(12 + 2 * dz, c).start()
        f_copy(13 + 2 * dz, c).start()

    def j_copy(n):
        dx, flip_low, half, to = HOPS[n]
        slot = at.f(dx, flip_low)
        where = pl.ds(0, 512) if half is None else pl.ds(half * 256, 256)
        src = int_ref.at[where] if (dx, flip_low) == (0, 0) else ib.at[slot, where]
        fit = {"low": low_peer, "core": core_peer, 1: at.f(1), -1: at.f(-1)}[to]
        return remote(src, ib.at[slot, where], js.at[n], jr.at[slot, half or 0], at.occ, fit)

    def j_send(*hops):
        for hop in hops:
            j_copy(HOPS.index(hop)).start()

    def j_got(slot, half):
        where = pl.ds(0, 512) if half is None else pl.ds(half * 256, 256)
        part = ib.at[slot, where]
        remote(part, part, js.at[0], jr.at[slot, half or 0], at.occ, at.fit).wait_recv()

    def j_own():
        for h in (0, 1):
            j_send((0, 0, h, -1), (0, 0, 1 - h, 1))
        j_send((0, 0, None, "core"))

    def j_low(h):
        j_got(at.f(0, 1), h)
        j_send((0, 1, h, -1), (0, 1, h, 1))
        if h == 1:
            j_send((0, 1, None, "core"))

    def j_relay(second, low):
        j_got(at.f(1, low), second)
        j_got(at.f(-1, low), 1 - second)
        if second:
            j_send((1, low, None, "core"), (-1, low, None, "core"))
        else:
            j_send((1, low, 0, -1), (-1, low, 1, 1))

    def j_last(low):
        j_got(at.f(2, low), 0)
        j_got(at.f(2, low), 1)
        j_send((2, low, None, "core"))

    def j_core():
        for low in (0, 1):
            for dx in (0, 1, -1, 2):
                j_got(at.f(dx, low, 1), None)

    def place(slot, c):
        if slot >= VIA:
            return spare.at[slot - VIA, :, pl.ds(pl.multiple_of((c % 2) * 128, 128), 128)]
        return pt.at[slot, :, rows(c)]

    def route(n, c):
        src, dst, dz, dy = ROUTES[n]
        return remote(place(src, c), place(dst, c), rs.at[n, c], rr.at[dst, c], at.o(dz, dy), at.fit)

    def send_on(slot, c, over_z=None):
        for n, (source, _, dz, _) in enumerate(ROUTES):
            if source == slot and over_z in (None, dz != 0):
                pl.when(takes(n, y, c))(lambda n=n: route(n, c).start())

    def got(slot, c):
        part = place(slot, c)
        remote(part, part, rs.at[0, 0], rr.at[slot, c], at.occ, at.fit).wait_recv()

    def energy_copy(d):
        k = SLOT[d]
        return remote(eb.at[0], eb.at[k], es.at[k], er.at[k], behind[d - 1], at.fit)

    def add(dy, c):
        def one(dz, carry):
            slot = at.o(dz, dy)
            acc[...] += dot_nn(fb[slot, rows(c)], ib[slot])
            return carry

        lax.fori_loop(0, 4, one, 0)

    def fit_most(c):
        if c == 0:
            j_core()
        acc[...] = jnp.zeros_like(acc)
        for dy in (0, 1, 3):
            add(dy, c)

    def fit_rest(c):
        for dz in range(4):
            f_got(dz, 2, c)
        add(2, c)
        whole = acc[...]
        hi = whole.astype(jnp.bfloat16)
        low = whole - hi.astype(jnp.float32)
        pt[0, 0, rows(c)] = hi
        pt[0, 1, rows(c)] = low.astype(jnp.bfloat16)
        ownt[0, :, rows(c)] = hi.astype(jnp.float32).T.astype(jnp.bfloat16)
        ownt[1, :, rows(c)] = low.T.astype(jnp.bfloat16)
        send_on(0, c, True)

    mine = pl.ds(pl.multiple_of(at.core * 256, 256), 256)
    other = pl.ds(pl.multiple_of((1 - at.core) * 256, 256), 256)

    def quarter(x):
        return pl.ds(pl.multiple_of(x * 64, 64), 64)

    def core_copy(k):
        return remote(pbo.at[k], cb.at[k], cs.at[k], cr.at[k], at.occ, core_peer)

    def x_copy(k, n):
        to = (at.x + (1, 3, 2)[n]) % 4
        if k in LOW_FIRST:
            src, dst = qz.at[k, pl.ds(pl.multiple_of(to * 32, 32), 32)], xb.at[k, n, pl.ds(0, 32)]
        else:
            src, dst = hb.at[k, quarter(to)], xb.at[k, n]
        return remote(src, dst, xs.at[k, n], xr.at[k, n], at.occ, x_peers[n])

    def half_of(low):
        return pl.ds(pl.multiple_of(low * 128, 128), 128)

    def z_copy(k):
        if k in LOW_FIRST:
            src, dst = hb.at[k, half_of(1 - at.low)], zz.at[k]
        else:
            half = pl.ds(pl.multiple_of((1 - at.low) * 32, 32), 32)
            src, dst = qb.at[k, half], zb.at[k]
        return remote(src, dst, zs.at[k], zr.at[k], at.occ, low_peer)

    def block(x, core):
        return pl.ds(pl.multiple_of(core * 256 + x * 64, 64), 64)

    def own_rows(k):
        if k in LOW_FIRST:
            start = at.core * 256 + at.low * 128 + at.x * 32
        else:
            start = at.core * 256 + at.x * 64 + at.low * 32
        return pl.ds(pl.multiple_of(start, 32), 32)

    def low_rows(low):
        return pl.ds(pl.multiple_of(at.core * 256 + low * 128, 128), 128)

    def az_copy(k):
        part = am.at[k, :, low_rows(at.low) if k in LOW_FIRST else own_rows(k)]
        return remote(part, part, azs.at[k], azr.at[k], at.occ, low_peer)

    def ax_copy(k, n):
        part = am.at[k, :, own_rows(k) if k in LOW_FIRST else block(at.x, at.core)]
        return remote(part, part, axs.at[k, n], axr.at[k, n], at.occ, x_peers[n])

    def ac_parts(k):
        return 2 if k in LOW_FIRST else 4

    def ac_copy(k, n):
        if k in LOW_FIRST:
            part = am.at[k, :, low_rows(at.low if n == 0 else 1 - at.low)]
        else:
            part = am.at[k, :, block((at.x + n) % 4, at.core)]
        return remote(part, part, acs.at[k, n], acr.at[k, n], at.occ, core_peer)

    def c1(k):
        if k == 5:
            for c in range(CHUNKS):
                got(SLOT[5], c)

        hi, lo = pt[k, 0], pt[k, 1]

        def part(where):
            return (
                dot_nn(ownt[0, where], hi) + dot_nn(ownt[0, where], lo) + dot_nn(ownt[1, where], hi)
            )

        pbo[k] = part(other)
        core_copy(k).start()
        hb[k] = part(mine)

    def start_x(copy, k):
        for n in range(3):
            copy(k, n).start()

    def wait_x(copy, k):
        for n in range(3):
            copy(k, n).wait_recv()

    def c2(k):
        core_copy(k).wait_recv()
        hb[k] += cb[k]
        if k in LOW_FIRST:
            z_copy(k).start()
        else:
            start_x(x_copy, k)

    def c3(k):
        if k in LOW_FIRST:
            z_copy(k).wait_recv()
            qz[k] = hb[k, half_of(at.low)] + zz[k]
            start_x(x_copy, k)
        else:
            wait_x(x_copy, k)
            qb[k] = (hb[k, quarter(at.x)] + xb[k, 0]) + (xb[k, 1] + xb[k, 2])
            z_copy(k).start()

    def c4(k):
        if k in LOW_FIRST:
            wait_x(x_copy, k)
            own = qz[k, pl.ds(pl.multiple_of(at.x * 32, 32), 32)]
            summed = (own + xb[k, 0, 0:32]) + (xb[k, 1, 0:32] + xb[k, 2, 0:32])
        else:
            z_copy(k).wait_recv()
            summed = qb[k, pl.ds(pl.multiple_of(at.low * 32, 32), 32)] + zb[k]
        energy = eb[0, 0:1, 0:1] + eb[k, 0:1, 0:1]
        denom = energy - vcol[own_rows(k), 0:1] - vir_ref[...]
        amplitude = summed / denom
        hi = amplitude.astype(jnp.bfloat16)
        am[k, 0, own_rows(k)] = hi
        am[k, 1, own_rows(k)] = (amplitude - hi.astype(jnp.float32)).astype(jnp.bfloat16)
        if k in LOW_FIRST:
            start_x(ax_copy, k)
        else:
            az_copy(k).start()

    def c5(k):
        if k in LOW_FIRST:
            wait_x(ax_copy, k)
            az_copy(k).start()
        else:
            az_copy(k).wait_recv()
            start_x(ax_copy, k)
        ac_copy(k, 0).start()

    def c6(k):
        if k in LOW_FIRST:
            az_copy(k).wait_recv()
            ac_copy(k, 1).start()
        else:
            for n in range(3):
                ax_copy(k, n).wait_recv()
                ac_copy(k, (3, 1, 2)[n]).start()

    def c7(k):
        for n in range(ac_parts(k)):
            ac_copy(k, n).wait_recv()
        hi, lo = pt[k, 0], pt[k, 1]
        out_ref[...] += dot_nt(hi, am[k, 0]) + dot_nt(hi, am[k, 1]) + dot_nt(lo, am[k, 0])
        energy = eb[0, 0:1, 0:1] + eb[k, 0:1, 0:1]
        total = jnp.zeros((1, 1), jnp.float32)
        for r in range(4):
            band = pl.ds(r * 128, 128)
            a = am[k, 0, band].astype(jnp.float32) + am[k, 1, band].astype(jnp.float32)
            b = am[k, 0, :, band].astype(jnp.float32) + am[k, 1, :, band].astype(jnp.float32)
            denom = energy - vcol[band, 0:1] - vir_ref[...]
            total += jnp.sum(a * denom * (2.0 * a - b.T), axis=(0, 1), keepdims=True)
        lane = lax.broadcasted_iota(jnp.int32, en_ref.shape, 1)
        en_ref[...] += jnp.where(lane == ORDER[k], total / (512 * 512), 0.0)

    def fill():
        fb[at.occ] = fit_ref[...]
        ib[at.fit] = int_ref[...]
        eb[0] = jnp.broadcast_to(occ_ref[...], (8, 128))
        out_ref[...] = jnp.zeros_like(out_ref)
        en_ref[...] = jnp.zeros_like(en_ref)
        vcol[...] = jnp.broadcast_to(vir_ref[...], (128, 512)).T
        for d in range(1, 6):
            energy_copy(d).start()

    def relay(d, c, only):
        slot = SLOT.get(d, {"V": VIA, "N": NEXT}.get(d))

        @pl.when(y == only)
        def _():
            got(slot, c)
            for n in range(len(ROUTES)):
                if ROUTES[n][0] == slot and takes(n, only, c):
                    route(n, c).start()

    def own_z(c):
        f_copy(0, c).start()
        f_copy(1, c).start()

    stages = {1: c1, 2: c2, 3: c3, 4: c4, 5: c5, 6: c6, 7: c7}
    steps = {
        "oz": own_z,
        "oy": lambda c: f_spread(0, c),
        "a1": lambda c: f_near(1, c),
        "a3": lambda c: f_near(3, c),
        "a2": f_far,
        "b": f_side,
        "jl": lambda h: j_send((0, 0, h, "low")),
        "jo": j_own,
        "jg": j_low,
        "jr": j_relay,
        "jt": j_last,
        "f1": fit_most,
        "f2": fit_rest,
        "py": lambda c: send_on(0, c, False),
        "g": relay,
        "c": lambda j, k: stages[j](k),
    }
    filled = False
    for name, *rest in PLAN:
        if not filled and name not in ("oz", "oy", "jl", "jo"):
            fill()
            filled = True
        if (name, *rest) == ("f2", 3):
            for d in range(1, 6):
                energy_copy(d).wait_recv()
        steps[name](*rest)

    for n in range(20):
        lax.fori_loop(0, CHUNKS, lambda c, _: (f_copy(n, c).wait_send(), _)[1], 0)
    for n in range(len(HOPS)):
        j_copy(n).wait_send()
    for n in range(len(ROUTES)):
        for c in range(CHUNKS):
            pl.when(takes(n, y, c))(lambda n=n, c=c: route(n, c).wait_send())
    for d in range(1, 6):
        energy_copy(d).wait_send()

    for k in range(6):
        core_copy(k).wait_send()
        z_copy(k).wait_send()
        az_copy(k).wait_send()
        for n in range(3):
            x_copy(k, n).wait_send()
            ax_copy(k, n).wait_send()
        for n in range(ac_parts(k)):
            ac_copy(k, n).wait_send()


def run(fitting, integrals, occ_energy, vir_energy):
    f32, bf16 = jnp.float32, jnp.bfloat16
    dma = pltpu.SemaphoreType.DMA
    return pl.pallas_call(
        kernel,
        out_shape=(
            jax.ShapeDtypeStruct((512, 512), f32),
            jax.ShapeDtypeStruct((1, STOPS), f32),
        ),
        in_specs=[pl.BlockSpec(memory_space=pltpu.VMEM)] * 4,
        out_specs=[pl.BlockSpec(memory_space=pltpu.VMEM)] * 2,
        scratch_shapes=[
            pltpu.VMEM((16, 512, 512), bf16),
            pltpu.VMEM((16, 512, 512), bf16),
            pltpu.VMEM((128, 512), f32),
            pltpu.VMEM((6, 2, 512, 512), bf16),
            pltpu.VMEM((2, 2, 256, 512), bf16),
            pltpu.VMEM((2, 512, 512), bf16),
            pltpu.VMEM((6, 256, 512), f32),
            pltpu.VMEM((6, 256, 512), f32),
            pltpu.VMEM((6, 256, 512), f32),
            pltpu.VMEM((6, 3, 64, 512), f32),
            pltpu.VMEM((6, 64, 512), f32),
            pltpu.VMEM((6, 32, 512), f32),
            pltpu.VMEM((6, 128, 512), f32),
            pltpu.VMEM((6, 128, 512), f32),
            pltpu.VMEM((6, 2, 512, 512), bf16),
            pltpu.VMEM((6, 8, 128), f32),
            pltpu.VMEM((512, 128), f32),
            dma((20, CHUNKS)), dma((16, CHUNKS, 2)),
            dma((len(HOPS),)), dma((16, 2)),
            dma((len(ROUTES), CHUNKS)), dma((8, CHUNKS)),
            dma((6,)), dma((6,)),
            dma((6,)), dma((6,)),
            dma((6, 3)), dma((6, 3)),
            dma((6,)), dma((6,)),
            dma((6,)), dma((6,)),
            dma((6, 3)), dma((6, 3)),
            dma((6, 4)), dma((6, 4)),
        ],
        compiler_params=pltpu.CompilerParams(
            collective_id=0, has_side_effects=True, vmem_limit_bytes=60 * 1024 * 1024
        ),
    )(fitting, integrals, occ_energy, vir_energy)


def body(integrals, fitting, occ_energy, vir_energy):
    density, energies = run(fitting, integrals[:, 0, :], occ_energy[:, None], vir_energy[None, :])
    return (density[:, None, :], energies)


def solution(mesh):
    placed = (P("fit", "occ", None), P("fit", "occ"), P("occ"), P())
    return jax.shard_map(
        body,
        mesh=mesh,
        in_specs=placed,
        out_specs=(P("fit", "occ", None), P("occ", None)),
        check_vma=False,
    )
```

```python
import jax
import jax.numpy as jnp
from jax import lax
from jax.experimental import pallas as pl
from jax.experimental.pallas import tpu as pltpu
from jax.sharding import PartitionSpec as P

STOPS = 6
MESH = pl.DeviceIdType.MESH


class Place:
    def __init__(self):
        self.occ = lax.axis_index("occ")
        self.fit = lax.axis_index("fit")
        self.z, self.y = self.occ // 4, self.occ % 4
        self.x, self.low, self.core = self.fit // 4, (self.fit // 2) % 2, self.fit % 2

    def o(self, dz, dy):
        return ((self.z + dz + 4) % 4) * 4 + (self.y + dy + 4) % 4

    def f(self, dx, flip_low=0, flip_core=0):
        low = self.low if not flip_low else 1 - self.low
        core = self.core if not flip_core else 1 - self.core
        return ((self.x + dx + 4) % 4) * 4 + low * 2 + core


def entry_barrier(peers):
    barrier = pltpu.get_barrier_semaphore()
    for occ, fit in peers:
        pl.semaphore_signal(barrier, inc=1, device_id={"occ": occ, "fit": fit}, device_id_type=MESH)
    pl.semaphore_wait(barrier, len(peers))


ORDER = (0, 4, 1, 3, 2, 5)
SLOT = {d: k for k, d in enumerate(ORDER)}
VIA, NEXT = 6, 7
CHUNKS = 4
ROUTES = (
    (0, SLOT[4], -1, 0),
    (0, SLOT[1], 0, -1),
    (0, SLOT[3], 0, 1),
    (0, VIA, 0, -1),
    (0, VIA, 1, 0),
    (SLOT[1], SLOT[2], 0, -1),
    (SLOT[4], SLOT[1], 0, -1),
    (SLOT[4], SLOT[3], 0, 1),
    (SLOT[4], SLOT[5], 0, -1),
    (SLOT[3], SLOT[2], 0, 1),
    (SLOT[2], SLOT[5], 0, 1),
    (VIA, NEXT, 1, 0),
    (NEXT, SLOT[5], 1, 0),
    (NEXT, SLOT[5], 0, -1),
)
HOPS = tuple((0, 0, h, to) for h in (0, 1) for to in ("low", 1, -1)) + tuple(
    (0, 1, h, to) for h in (0, 1) for to in (1, -1)
) + ((0, 0, None, "core"), (0, 1, None, "core")) + tuple(
    hop
    for low in (0, 1)
    for hop in (
        (1, low, 0, -1),
        (-1, low, 1, 1),
        (1, low, None, "core"),
        (-1, low, None, "core"),
        (2, low, None, "core"),
    )
)
LOW_FIRST = (2, 4)
PLAN = (
    ("oy", 2), ("oy", 1), ("oz", 0), ("oy", 0), ("jo",), ("jl", 0), ("jl", 1), ("oz", 1), ("oy", 3),
    ("jr", 0, 0), ("oz", 2), ("a3", 0), ("a1", 0), ("jg", 0), ("oz", 3), ("a1", 1), ("b", 0, 0),
    ("b", 0, 1), ("b", 0, 3), ("b", 3, 0), ("jt", 0), ("jg", 1), ("b", 1, 1), ("a3", 1), ("a1", 3),
    ("jr", 0, 1), ("a3", 2), ("jr", 1, 1), ("jr", 1, 0), ("a2", 0), ("b", 3, 1), ("b", 1, 0),
    ("jt", 1), ("b", 2, 0), ("b", 0, 2), ("a1", 2), ("f1", 0), ("a2", 1), ("f2", 0), ("a2", 2),
    ("b", 2, 1), ("a3", 3), ("b", 3, 2), ("b", 1, 2), ("f1", 1), ("f2", 1), ("a2", 3), ("b", 2, 2),
    ("b", 1, 3), ("py", 0), ("b", 3, 3), ("f1", 2), ("g", 4, 0, 1), ("b", 2, 3), ("py", 1),
    ("g", 4, 0, 0), ("f2", 2), ("g", 4, 0, 2), ("g", "V", 0, 3), ("f1", 3), ("g", 4, 1, 1),
    ("g", 3, 0, 2), ("g", 4, 1, 0), ("f2", 3), ("py", 2), ("g", "V", 1, 3), ("g", 3, 0, 0),
    ("g", 1, 0, 2), ("g", 3, 0, 1), ("c", 1, 0), ("g", 4, 1, 3), ("py", 3), ("g", 3, 1, 0),
    ("g", 4, 1, 2), ("g", 1, 0, 0), ("g", 3, 1, 1), ("c", 2, 0), ("g", 2, 0, 3), ("g", "V", 2, 0),
    ("g", 4, 2, 2), ("g", 4, 2, 1), ("g", 4, 0, 3), ("g", 4, 2, 3), ("g", 3, 1, 2), ("g", 1, 2, 0),
    ("g", "N", 0, 3), ("g", 1, 0, 1), ("g", 4, 2, 0), ("g", 1, 1, 1), ("g", 2, 1, 2),
    ("g", 3, 0, 3), ("g", 1, 2, 1), ("c", 3, 0), ("g", 4, 3, 3), ("g", 4, 3, 0), ("g", 4, 3, 1),
    ("g", 1, 2, 2), ("g", 4, 3, 2), ("c", 1, 1), ("c", 2, 1), ("g", 1, 3, 0), ("g", 1, 3, 1),
    ("g", 3, 2, 1), ("g", 1, 1, 2), ("g", 1, 1, 3), ("g", 1, 3, 2), ("g", 1, 2, 3), ("g", 3, 3, 0),
    ("g", 3, 2, 0), ("g", 3, 2, 2), ("g", 1, 0, 3), ("c", 4, 0), ("g", 3, 1, 3), ("g", 1, 3, 3),
    ("g", 1, 1, 0), ("c", 1, 2), ("g", "N", 1, 3), ("g", 3, 3, 3), ("g", 3, 3, 2), ("g", 3, 2, 3),
    ("g", 2, 0, 0), ("g", 2, 1, 3), ("g", 2, 0, 2), ("c", 5, 0), ("g", 3, 3, 1), ("g", 2, 1, 1),
    ("c", 2, 2), ("g", "V", 3, 0), ("c", 1, 3), ("c", 2, 3), ("c", 3, 1), ("g", 2, 0, 1),
    ("g", 2, 2, 3), ("c", 3, 2), ("g", 2, 2, 2), ("g", 2, 2, 0), ("c", 6, 0), ("c", 4, 1),
    ("g", 2, 2, 1), ("g", 2, 3, 2), ("g", "N", 2, 0), ("g", 2, 3, 0), ("g", 2, 3, 3),
    ("g", 2, 1, 0), ("g", 2, 3, 1), ("c", 1, 4), ("g", "N", 3, 0), ("c", 2, 4), ("c", 5, 1),
    ("c", 4, 2), ("c", 3, 3), ("c", 1, 5), ("c", 3, 4), ("c", 4, 3), ("c", 2, 5), ("c", 5, 2),
    ("c", 6, 1), ("c", 4, 4), ("c", 7, 1), ("c", 6, 2), ("c", 3, 5), ("c", 5, 3), ("c", 4, 5),
    ("c", 5, 4), ("c", 5, 5), ("c", 7, 2), ("c", 6, 3), ("c", 7, 0), ("c", 6, 4), ("c", 7, 3),
    ("c", 6, 5), ("c", 7, 4), ("c", 7, 5),
)


def carries(y, c):
    return ((y == 3) & (c < 2)) | ((y == 0) & (c >= 2))


def takes(route, y, c):
    return (
        True,
        y > 0,
        y == 3,
        (y == 0) & (c < 2),
        (y == 0) & (c >= 2),
        y == 1,
        y == 0,
        y < 3,
        y >= 2,
        y < 3,
        y == 3,
        carries(y, c),
        (y == 3) & (c < 2),
        (y == 0) & (c >= 2),
    )[route]


def dot_nt(a, b):
    return lax.dot_general(a, b, (((1,), (1,)), ((), ())), preferred_element_type=jnp.float32)


def dot_nn(a, b):
    return jnp.dot(a, b, preferred_element_type=jnp.float32)


def kernel(
    fit_ref, int_ref, occ_ref, vir_ref, out_ref, en_ref,
    fb, ib, acc, pt, spare, ownt, pbo, hb, cb, xb, qb, zb, qz, zz, am, eb, vcol, dens,
    fs, fr, js, jr, rs, rr, es, er, cs, cr, xs, xr, zs, zr, azs, azr, axs, axr, acs, acr,
):
    at = Place()
    y = at.y
    core_peer, low_peer = at.f(0, 0, 1), at.f(0, 1)
    x_peers = (at.f(1), at.f(-1), at.f(2))
    ahead = [(at.occ + d) % 16 for d in range(1, 6)]
    behind = [(at.occ + 16 - d) % 16 for d in range(1, 6)]
    entry_barrier(
        [(o, at.fit) for o in ahead + behind]
        + [(at.occ, f) for f in x_peers + (core_peer, low_peer)]
    )

    def remote(src, dst, ssem, rsem, occ, fit):
        return pltpu.make_async_remote_copy(
            src_ref=src, dst_ref=dst, send_sem=ssem, recv_sem=rsem,
            device_id={"occ": occ, "fit": fit}, device_id_type=MESH,
        )

    def rows(c):
        return pl.ds(pl.multiple_of(c * 128, 128), 128)

    def rows_of(c, half):
        if half is None:
            return rows(c)
        return pl.ds(pl.multiple_of(c * 128 + half * 64, 64), 64)

    def f_copy(n, c):
        if n < 2:
            slot, half, own, to = at.occ, None, True, at.o((1, -1)[n], 0)
        elif n < 4:
            slot, half, own, to = at.o((1, -1)[n - 2], 0), n - 2, False, at.o((-1, 1)[n - 2], 0)
        elif n < 12:
            dz, up = (n - 4) // 2, (n - 4) % 2
            slot, half, own, to = at.o(dz, 0), None, dz == 0, at.o(0, (1, -1)[up])
        else:
            dz, up = (n - 12) // 2, (n - 12) % 2
            slot, half, own, to = at.o(dz, (1, -1)[up]), up, False, at.o(0, (-1, 1)[up])
        where = rows_of(c, half)
        src = fit_ref.at[where] if own else fb.at[slot, where]
        return remote(src, fb.at[slot, where], fs.at[n, c], fr.at[slot, c, half or 0], to, at.fit)

    def f_got(dz, dy, c):
        slot = at.o(dz, dy)
        for half in ((0, 1) if dy == 2 or (dz == 2 and dy == 0) else (None,)):
            part = fb.at[slot, rows_of(c, half)]
            remote(part, part, fs.at[0, 0], fr.at[slot, c, half or 0], at.occ, at.fit).wait_recv()

    def f_spread(dz, c):
        f_copy(4 + 2 * dz, c).start()
        f_copy(5 + 2 * dz, c).start()

    def f_near(dz, c):
        f_got(dz, 0, c)
        f_copy(2 if dz == 1 else 3, c).start()
        f_spread(dz, c)

    def f_far(c):
        f_got(2, 0, c)
        f_spread(2, c)

    def f_side(dz, c):
        f_got(dz, 1, c)
        f_got(dz, 3, c)
        f_copy(12 + 2 * dz, c).start()
        f_copy(13 + 2 * dz, c).start()

    def j_copy(n):
        dx, flip_low, half, to = HOPS[n]
        slot = at.f(dx, flip_low)
        where = pl.ds(0, 512) if half is None else pl.ds(half * 256, 256)
        src = int_ref.at[where] if (dx, flip_low) == (0, 0) else ib.at[slot, where]
        fit = {"low": low_peer, "core": core_peer, 1: at.f(1), -1: at.f(-1)}[to]
        return remote(src, ib.at[slot, where], js.at[n], jr.at[slot, half or 0], at.occ, fit)

    def j_send(*hops):
        for hop in hops:
            j_copy(HOPS.index(hop)).start()

    def j_got(slot, half):
        where = pl.ds(0, 512) if half is None else pl.ds(half * 256, 256)
        part = ib.at[slot, where]
        remote(part, part, js.at[0], jr.at[slot, half or 0], at.occ, at.fit).wait_recv()

    def j_own():
        for h in (0, 1):
            j_send((0, 0, h, -1), (0, 0, 1 - h, 1))
        j_send((0, 0, None, "core"))

    def j_low(h):
        j_got(at.f(0, 1), h)
        j_send((0, 1, h, -1), (0, 1, h, 1))
        if h == 1:
            j_send((0, 1, None, "core"))

    def j_relay(second, low):
        j_got(at.f(1, low), second)
        j_got(at.f(-1, low), 1 - second)
        if second:
            j_send((1, low, None, "core"), (-1, low, None, "core"))
        else:
            j_send((1, low, 0, -1), (-1, low, 1, 1))

    def j_last(low):
        j_got(at.f(2, low), 0)
        j_got(at.f(2, low), 1)
        j_send((2, low, None, "core"))

    def j_core():
        for low in (0, 1):
            for dx in (0, 1, -1, 2):
                j_got(at.f(dx, low, 1), None)

    def place(slot, c):
        if slot >= VIA:
            return spare.at[slot - VIA, :, pl.ds(pl.multiple_of((c % 2) * 128, 128), 128)]
        return pt.at[slot, :, rows(c)]

    def route(n, c):
        src, dst, dz, dy = ROUTES[n]
        return remote(place(src, c), place(dst, c), rs.at[n, c], rr.at[dst, c], at.o(dz, dy), at.fit)

    def send_on(slot, c, over_z=None):
        for n, (source, _, dz, _) in enumerate(ROUTES):
            if source == slot and over_z in (None, dz != 0):
                pl.when(takes(n, y, c))(lambda n=n: route(n, c).start())

    def got(slot, c):
        part = place(slot, c)
        remote(part, part, rs.at[0, 0], rr.at[slot, c], at.occ, at.fit).wait_recv()

    def energy_copy(d):
        k = SLOT[d]
        return remote(eb.at[0], eb.at[k], es.at[k], er.at[k], behind[d - 1], at.fit)

    def add(dy, c):
        def one(dz, carry):
            slot = at.o(dz, dy)
            acc[...] += dot_nn(fb[slot, rows(c)], ib[slot])
            return carry

        lax.fori_loop(0, 4, one, 0)

    def fit_most(c):
        if c == 0:
            j_core()
        acc[...] = jnp.zeros_like(acc)
        for dy in (0, 1, 3):
            add(dy, c)

    def fit_rest(c):
        for dz in range(4):
            f_got(dz, 2, c)
        add(2, c)
        whole = acc[...]
        hi = whole.astype(jnp.bfloat16)
        low = whole - hi.astype(jnp.float32)
        pt[0, 0, rows(c)] = hi
        pt[0, 1, rows(c)] = low.astype(jnp.bfloat16)
        ownt[0, :, rows(c)] = hi.astype(jnp.float32).T.astype(jnp.bfloat16)
        ownt[1, :, rows(c)] = low.T.astype(jnp.bfloat16)
        send_on(0, c, True)

    mine = pl.ds(pl.multiple_of(at.core * 256, 256), 256)
    other = pl.ds(pl.multiple_of((1 - at.core) * 256, 256), 256)

    def quarter(x):
        return pl.ds(pl.multiple_of(x * 64, 64), 64)

    def core_copy(k):
        return remote(pbo.at[k], cb.at[k], cs.at[k], cr.at[k], at.occ, core_peer)

    def x_copy(k, n):
        to = (at.x + (1, 3, 2)[n]) % 4
        if k in LOW_FIRST:
            src, dst = qz.at[k, pl.ds(pl.multiple_of(to * 32, 32), 32)], xb.at[k, n, pl.ds(0, 32)]
        else:
            src, dst = hb.at[k, quarter(to)], xb.at[k, n]
        return remote(src, dst, xs.at[k, n], xr.at[k, n], at.occ, x_peers[n])

    def half_of(low):
        return pl.ds(pl.multiple_of(low * 128, 128), 128)

    def z_copy(k):
        if k in LOW_FIRST:
            src, dst = hb.at[k, half_of(1 - at.low)], zz.at[k]
        else:
            half = pl.ds(pl.multiple_of((1 - at.low) * 32, 32), 32)
            src, dst = qb.at[k, half], zb.at[k]
        return remote(src, dst, zs.at[k], zr.at[k], at.occ, low_peer)

    def block(x, core):
        return pl.ds(pl.multiple_of(core * 256 + x * 64, 64), 64)

    def own_rows(k):
        if k in LOW_FIRST:
            start = at.core * 256 + at.low * 128 + at.x * 32
        else:
            start = at.core * 256 + at.x * 64 + at.low * 32
        return pl.ds(pl.multiple_of(start, 32), 32)

    def low_rows(low):
        return pl.ds(pl.multiple_of(at.core * 256 + low * 128, 128), 128)

    def az_copy(k):
        part = am.at[k, :, low_rows(at.low) if k in LOW_FIRST else own_rows(k)]
        return remote(part, part, azs.at[k], azr.at[k], at.occ, low_peer)

    def ax_copy(k, n):
        part = am.at[k, :, own_rows(k) if k in LOW_FIRST else block(at.x, at.core)]
        return remote(part, part, axs.at[k, n], axr.at[k, n], at.occ, x_peers[n])

    def ac_parts(k):
        return 2 if k in LOW_FIRST else 4

    def ac_copy(k, n):
        if k in LOW_FIRST:
            part = am.at[k, :, low_rows(at.low if n == 0 else 1 - at.low)]
        else:
            part = am.at[k, :, block((at.x + n) % 4, at.core)]
        return remote(part, part, acs.at[k, n], acr.at[k, n], at.occ, core_peer)

    def c1(k):
        if k == 5:
            for c in range(CHUNKS):
                got(SLOT[5], c)

        hi, lo = pt[k, 0], pt[k, 1]

        def part(where):
            return (
                dot_nn(ownt[0, where], hi) + dot_nn(ownt[0, where], lo) + dot_nn(ownt[1, where], hi)
            )

        pbo[k] = part(other)
        core_copy(k).start()
        hb[k] = part(mine)

    def start_x(copy, k):
        for n in range(3):
            copy(k, n).start()

    def wait_x(copy, k):
        for n in range(3):
            copy(k, n).wait_recv()

    def c2(k):
        core_copy(k).wait_recv()
        hb[k] += cb[k]
        if k in LOW_FIRST:
            z_copy(k).start()
        else:
            start_x(x_copy, k)

    def c3(k):
        if k in LOW_FIRST:
            z_copy(k).wait_recv()
            qz[k] = hb[k, half_of(at.low)] + zz[k]
            start_x(x_copy, k)
        else:
            wait_x(x_copy, k)
            qb[k] = (hb[k, quarter(at.x)] + xb[k, 0]) + (xb[k, 1] + xb[k, 2])
            z_copy(k).start()

    def c4(k):
        if k in LOW_FIRST:
            wait_x(x_copy, k)
            own = qz[k, pl.ds(pl.multiple_of(at.x * 32, 32), 32)]
            summed = (own + xb[k, 0, 0:32]) + (xb[k, 1, 0:32] + xb[k, 2, 0:32])
        else:
            z_copy(k).wait_recv()
            summed = qb[k, pl.ds(pl.multiple_of(at.low * 32, 32), 32)] + zb[k]
        energy = eb[0, 0:1, 0:1] + eb[k, 0:1, 0:1]
        denom = energy - vcol[own_rows(k), 0:1] - vir_ref[...]
        amplitude = summed / denom
        hi = amplitude.astype(jnp.bfloat16)
        am[k, 0, own_rows(k)] = hi
        am[k, 1, own_rows(k)] = (amplitude - hi.astype(jnp.float32)).astype(jnp.bfloat16)
        if k in LOW_FIRST:
            start_x(ax_copy, k)
        else:
            az_copy(k).start()

    def c5(k):
        if k in LOW_FIRST:
            wait_x(ax_copy, k)
            az_copy(k).start()
        else:
            az_copy(k).wait_recv()
            start_x(ax_copy, k)
        ac_copy(k, 0).start()

    def c6(k):
        if k in LOW_FIRST:
            az_copy(k).wait_recv()
            ac_copy(k, 1).start()
        else:
            for n in range(3):
                ax_copy(k, n).wait_recv()
                ac_copy(k, (3, 1, 2)[n]).start()

    def c7(k):
        for n in range(ac_parts(k)):
            ac_copy(k, n).wait_recv()
        hi, lo = pt[k, 0], pt[k, 1]
        dens[...] += dot_nt(hi, am[k, 0]) + dot_nt(hi, am[k, 1]) + dot_nt(lo, am[k, 0])
        energy = eb[0, 0:1, 0:1] + eb[k, 0:1, 0:1]
        total = jnp.zeros((1, 1), jnp.float32)
        for r in range(4):
            band = pl.ds(r * 128, 128)
            a = am[k, 0, band].astype(jnp.float32) + am[k, 1, band].astype(jnp.float32)
            b = am[k, 0, :, band].astype(jnp.float32) + am[k, 1, :, band].astype(jnp.float32)
            denom = energy - vcol[band, 0:1] - vir_ref[...]
            total += jnp.sum(a * denom * (2.0 * a - b.T), axis=(0, 1), keepdims=True)
        lane = lax.broadcasted_iota(jnp.int32, en_ref.shape, 1)
        en_ref[...] += jnp.where(lane == ORDER[k], total / (512 * 512), 0.0)

    def fill():
        fb[at.occ] = fit_ref[...]
        ib[at.fit] = int_ref[...]
        eb[0] = jnp.broadcast_to(occ_ref[...], (8, 128))
        dens[...] = jnp.zeros_like(dens)
        en_ref[...] = jnp.zeros_like(en_ref)
        vcol[...] = jnp.broadcast_to(vir_ref[...], (128, 512)).T
        for d in range(1, 6):
            energy_copy(d).start()

    def relay(d, c, only):
        slot = SLOT.get(d, {"V": VIA, "N": NEXT}.get(d))

        @pl.when(y == only)
        def _():
            got(slot, c)
            for n in range(len(ROUTES)):
                if ROUTES[n][0] == slot and takes(n, only, c):
                    route(n, c).start()

    def own_z(c):
        f_copy(0, c).start()
        f_copy(1, c).start()

    stages = {1: c1, 2: c2, 3: c3, 4: c4, 5: c5, 6: c6, 7: c7}
    steps = {
        "oz": own_z,
        "oy": lambda c: f_spread(0, c),
        "a1": lambda c: f_near(1, c),
        "a3": lambda c: f_near(3, c),
        "a2": f_far,
        "b": f_side,
        "jl": lambda h: j_send((0, 0, h, "low")),
        "jo": j_own,
        "jg": j_low,
        "jr": j_relay,
        "jt": j_last,
        "f1": fit_most,
        "f2": fit_rest,
        "py": lambda c: send_on(0, c, False),
        "g": relay,
        "c": lambda j, k: stages[j](k),
    }
    filled = False
    for name, *rest in PLAN:
        if not filled and name not in ("oz", "oy", "jl", "jo"):
            fill()
            filled = True
        if (name, *rest) == ("f2", 3):
            for d in range(1, 6):
                energy_copy(d).wait_recv()
        steps[name](*rest)

    out_ref[:, 0, :] = dens[...]
    for n in range(20):
        lax.fori_loop(0, CHUNKS, lambda c, _: (f_copy(n, c).wait_send(), _)[1], 0)
    for n in range(len(HOPS)):
        j_copy(n).wait_send()
    for n in range(len(ROUTES)):
        for c in range(CHUNKS):
            pl.when(takes(n, y, c))(lambda n=n, c=c: route(n, c).wait_send())
    for d in range(1, 6):
        energy_copy(d).wait_send()

    for k in range(6):
        core_copy(k).wait_send()
        z_copy(k).wait_send()
        az_copy(k).wait_send()
        for n in range(3):
            x_copy(k, n).wait_send()
            ax_copy(k, n).wait_send()
        for n in range(ac_parts(k)):
            ac_copy(k, n).wait_send()


def run(fitting, integrals, occ_energy, vir_energy):
    f32, bf16 = jnp.float32, jnp.bfloat16
    dma = pltpu.SemaphoreType.DMA
    return pl.pallas_call(
        kernel,
        out_shape=(
            jax.ShapeDtypeStruct((512, 1, 512), f32),
            jax.ShapeDtypeStruct((1, STOPS), f32),
        ),
        in_specs=[pl.BlockSpec(memory_space=pltpu.VMEM)] * 4,
        out_specs=[pl.BlockSpec(memory_space=pltpu.VMEM)] * 2,
        scratch_shapes=[
            pltpu.VMEM((16, 512, 512), bf16),
            pltpu.VMEM((16, 512, 512), bf16),
            pltpu.VMEM((128, 512), f32),
            pltpu.VMEM((6, 2, 512, 512), bf16),
            pltpu.VMEM((2, 2, 256, 512), bf16),
            pltpu.VMEM((2, 512, 512), bf16),
            pltpu.VMEM((6, 256, 512), f32),
            pltpu.VMEM((6, 256, 512), f32),
            pltpu.VMEM((6, 256, 512), f32),
            pltpu.VMEM((6, 3, 64, 512), f32),
            pltpu.VMEM((6, 64, 512), f32),
            pltpu.VMEM((6, 32, 512), f32),
            pltpu.VMEM((6, 128, 512), f32),
            pltpu.VMEM((6, 128, 512), f32),
            pltpu.VMEM((6, 2, 512, 512), bf16),
            pltpu.VMEM((6, 8, 128), f32),
            pltpu.VMEM((512, 128), f32),
            pltpu.VMEM((512, 512), f32),
            dma((20, CHUNKS)), dma((16, CHUNKS, 2)),
            dma((len(HOPS),)), dma((16, 2)),
            dma((len(ROUTES), CHUNKS)), dma((8, CHUNKS)),
            dma((6,)), dma((6,)),
            dma((6,)), dma((6,)),
            dma((6, 3)), dma((6, 3)),
            dma((6,)), dma((6,)),
            dma((6,)), dma((6,)),
            dma((6, 3)), dma((6, 3)),
            dma((6, 4)), dma((6, 4)),
        ],
        compiler_params=pltpu.CompilerParams(
            collective_id=0, has_side_effects=True, vmem_limit_bytes=60 * 1024 * 1024
        ),
    )(fitting, integrals, occ_energy, vir_energy)


def body(integrals, fitting, occ_energy, vir_energy):
    density, energies = run(fitting, integrals[:, 0, :], occ_energy[:, None], vir_energy[None, :])
    return (density, energies)


def solution(mesh):
    placed = (P("fit", "occ", None), P("fit", "occ"), P("occ"), P())
    return jax.shard_map(
        body,
        mesh=mesh,
        in_specs=placed,
        out_specs=(P("fit", "occ", None), P("occ", None)),
        check_vma=False,
    )
```
